512 devices in a mesh: inp: 8 (over z_lo), out: 8 (over y, z_hi), tok: 8 (over x, core).
Axes of the slice: x: 4, y: 4, z: 16 (z_hi: 2, z_lo: 8; z = z_hi * 8 + z_lo), core: 2. Of those that a mesh axis runs over, the one named last changes fastest.
Arguments:
- saved_input: float32 [1024, 4096], P('tok', 'inp'), may hold values from -6 to 6
- saved_gate: float32 [1024, 28672], P('inp', ('out', 'tok')), may hold values from -6 to 6
- saved_up: float32 [1024, 28672], P('inp', ('out', 'tok')), may hold values from -6 to 6
- out_grad: bfloat16 [1024, 4096], P('tok', 'inp'), may hold values from -1.5 to 1.5
- w_gate: bfloat16 [4096, 28672], P('inp', ('out', 'tok')), may hold values from -0.09375 to 0.09375
- w_up: bfloat16 [4096, 28672], P('inp', ('out', 'tok')), may hold values from -0.09375 to 0.09375
- w_down: bfloat16 [28672, 4096], P(('out', 'tok'), 'inp'), may hold values from -0.03125 to 0.03125
Outputs:
- input_grad: bfloat16 [1024, 4096], P(('out', 'tok'), 'inp')
- gate_wgrad: bfloat16 [4096, 28672], P('inp', ('out', 'tok'))
- up_wgrad: bfloat16 [4096, 28672], P('inp', ('out', 'tok'))
- down_wgrad: bfloat16 [28672, 4096], P(('out', 'tok'), 'inp')
The draws below stay inside these ranges and needn't reach their ends.
All inputs are finite; a program needn't handle non-finite values.
Results may differ from the reference program's by a relative error of at most 0.0057.
Values may be sent and summed in bfloat16 or wider, within the bound.
A program may use at most 64 MiB of HBM per device.

```python
import jax
import jax.numpy as jnp

D = 4096
FF = 28672
TOKENS = 1024


def block_levels(own_key, shape, cuts, least, top_value):
    factor_of, own = 1.0, jax.random.fold_in(own_key, 6)
    for axis_at, blocks in cuts:
        steps = jnp.exp(jax.random.uniform(jax.random.fold_in(own, axis_at), (blocks,), jnp.float32, least / len(cuts), top_value / len(cuts)))
        factor_of = factor_of * jnp.repeat(steps, shape[axis_at] // blocks).reshape([-1 if axis == axis_at else 1 for axis in range(len(shape))])
    return factor_of


def bell_draw(key, shape, scale, bound, pieces=(), kind=jnp.bfloat16):
    level = block_levels(key, shape, pieces, -0.22, 0.18) if pieces else 1.0
    array = jax.random.normal(key, shape, jnp.float32) * scale * level
    return jnp.minimum(jnp.maximum(array, -bound), bound).astype(kind)


def setup_inputs(seed: int = 0) -> dict:
    streams_of = jax.random.split(jax.random.key(seed), 8)
    saved_input = bell_draw(streams_of[0], (TOKENS, D), 1.0, 6.0, ((0, 8), (1, 8)), jnp.float32)
    saved_gate = bell_draw(streams_of[1], (TOKENS, FF), 1.0, 6.0, ((0, 8), (1, 64)), jnp.float32)
    saved_up = bell_draw(streams_of[2], (TOKENS, FF), 1.0, 6.0, ((0, 8), (1, 64)), jnp.float32)
    out_grad = bell_draw(streams_of[3], (TOKENS, D), 0.25, 1.5, ((0, 8), (1, 8)))
    w_gate = bell_draw(streams_of[4], (D, FF), D ** -0.5, 0.09375, ((0, 8), (1, 64)))
    w_up = bell_draw(streams_of[5], (D, FF), D ** -0.5, 0.09375, ((0, 8), (1, 64)))
    w_down = bell_draw(streams_of[6], (FF, D), FF ** -0.5, 0.03125, ((0, 64), (1, 8)))
    return {"saved_input": saved_input, "saved_gate": saved_gate, "saved_up": saved_up, "out_grad": out_grad, "w_gate": w_gate, "w_up": w_up, "w_down": w_down}


def reference(saved_input, saved_gate, saved_up, out_grad, w_gate, w_up, w_down):
    input_b = saved_input.astype(jnp.bfloat16)
    hidden_grad = jnp.dot(out_grad, w_down.T, preferred_element_type=jnp.float32)
    sig = jax.nn.sigmoid(saved_gate)
    hidden = (saved_gate * sig * saved_up).astype(jnp.bfloat16)
    gate_grad = (hidden_grad * saved_up * sig * (1.0 + saved_gate * (1.0 - sig))).astype(jnp.bfloat16)
    up_grad = (hidden_grad * saved_gate * sig).astype(jnp.bfloat16)
    gate_wgrad = jnp.dot(input_b.T, gate_grad, preferred_element_type=jnp.float32).astype(jnp.bfloat16)
    up_wgrad = jnp.dot(input_b.T, up_grad, preferred_element_type=jnp.float32).astype(jnp.bfloat16)
    down_wgrad = jnp.dot(hidden.T, out_grad, preferred_element_type=jnp.float32).astype(jnp.bfloat16)
    total = jnp.dot(gate_grad, w_gate.T, preferred_element_type=jnp.float32)
    total = total + jnp.dot(up_grad, w_up.T, preferred_element_type=jnp.float32)
    input_grad = total.astype(jnp.bfloat16)
    return input_grad, gate_wgrad, up_wgrad, down_wgrad
```

```python
import jax
import jax.numpy as jnp
from jax import lax
from jax.sharding import PartitionSpec as P


def local_terms(hidden_grad, gate_vals, up_vals):
    sig = jax.nn.sigmoid(gate_vals)
    hidden = (gate_vals * sig * up_vals).astype(jnp.bfloat16)
    gate_grad = (hidden_grad * up_vals * sig * (1.0 + gate_vals * (1.0 - sig))).astype(jnp.bfloat16)
    up_grad = (hidden_grad * gate_vals * sig).astype(jnp.bfloat16)
    return (gate_grad, up_grad, hidden)


def local(saved_input, saved_gate, saved_up, out_grad, w_gate, w_up, w_down):
    last_dims = (((1,), (1,)), ((), ()))
    lead_dims = (((0,), (0,)), ((), ()))
    input_b = saved_input.astype(jnp.bfloat16)
    all_grads = lax.all_gather(out_grad, "tok", axis=0, tiled=True)
    all_inputs = lax.all_gather(input_b, "tok", axis=0, tiled=True)
    partial_sum = lax.dot_general(all_grads, w_down, last_dims, preferred_element_type=jnp.float32)
    hidden_grad = lax.psum_scatter(partial_sum, "inp", scatter_dimension=0, tiled=True)
    gate_grad, up_grad, hidden = local_terms(hidden_grad, saved_gate, saved_up)
    gate_grad = lax.all_gather(gate_grad, "inp", axis=0, tiled=True)
    up_grad = lax.all_gather(up_grad, "inp", axis=0, tiled=True)
    hidden = lax.all_gather(hidden, "inp", axis=0, tiled=True)
    gate_wgrad = lax.dot_general(
        all_inputs, gate_grad, lead_dims, preferred_element_type=jnp.float32
    ).astype(jnp.bfloat16)
    up_wgrad = lax.dot_general(
        all_inputs, up_grad, lead_dims, preferred_element_type=jnp.float32
    ).astype(jnp.bfloat16)
    down_wgrad = lax.dot_general(
        hidden, all_grads, lead_dims, preferred_element_type=jnp.float32
    ).astype(jnp.bfloat16)
    result = lax.dot_general(gate_grad, w_gate, last_dims, preferred_element_type=jnp.float32)
    result = result + lax.dot_general(up_grad, w_up, last_dims, preferred_element_type=jnp.float32)
    tokens, width = result.shape
    outs, toks = lax.axis_size("out"), lax.axis_size("tok")
    rows = tokens // (outs * toks)
    result = result.reshape(outs, toks, rows, width).transpose(1, 0, 2, 3).reshape(tokens, width)
    summed = lax.psum_scatter(result, "tok", scatter_dimension=0, tiled=True)
    summed = lax.psum_scatter(summed, "out", scatter_dimension=0, tiled=True)
    return (summed.astype(jnp.bfloat16), gate_wgrad, up_wgrad, down_wgrad)


def solution(mesh):
    placed = (
        P("tok", "inp"),
        P("inp", ("out", "tok")),
        P("inp", ("out", "tok")),
        P("tok", "inp"),
        P("inp", ("out", "tok")),
        P("inp", ("out", "tok")),
        P(("out", "tok"), "inp"),
    )
    return jax.shard_map(
        local,
        mesh=mesh,
        in_specs=placed,
        out_specs=(
            P(("out", "tok"), "inp"),
            P("inp", ("out", "tok")),
            P("inp", ("out", "tok")),
            P(("out", "tok"), "inp"),
        ),
        check_vma=False,
    )
```

```python
import functools

import jax
import jax.numpy as jnp
from jax import lax
from jax.experimental import pallas as pl
from jax.experimental.pallas import tpu as pltpu
from jax.sharding import PartitionSpec as P

MESH = pl.DeviceIdType.MESH
F32 = jnp.float32
BF16 = jnp.bfloat16
LAST = (((1,), (1,)), ((), ()))
LEAD = (((0,), (0,)), ((), ()))
NC = 2
NZ = 2


def dot(a, b, dims=(((1,), (0,)), ((), ()))):
    return lax.dot_general(a, b, dims, preferred_element_type=F32)


def kernel(
    sizes,
    x_ref, g_ref, u_ref, go_ref, wg_ref, wu_ref, wd_ref,
    ig_ref, gw_ref, uw_ref, dw_ref,
    GA, XA, GU, H, RU, RD, PS, TA, TB, GW, UW, DW, IG2, IGR, XS, XR, YS, YR, ZR,
    ga_s, ga_r, xa_s, xa_r, gu_s, gu_r, h_s, h_r, ru_s, ru_r, rd_s, rd_r,
    ig_s, ig_r, xs_s, xs_r, ys_s, ys_r, z_s, z_r,
):
    NI, NO, NT = sizes
    NX, NY = NT // NC, NO // NZ
    zi, o, t = lax.axis_index("inp"), lax.axis_index("out"), lax.axis_index("tok")
    x, core = t // NC, t % NC
    y, zh = o // NZ, o % NZ
    F, tb = g_ref.shape
    ts, D = go_ref.shape
    rows = tb // NT

    def at_inp(k):
        return {"inp": k}

    def at_tok(k):
        return {"tok": k}

    def at_out(k):
        return {"out": k}

    def rc(src, dst, ss, rs, dev):
        return pltpu.make_async_remote_copy(
            src_ref=src, dst_ref=dst, send_sem=ss, recv_sem=rs, device_id=dev, device_id_type=MESH
        )

    has_up, has_dn = zi < NI - 1, zi > 0
    sib = x * NC + (1 - core)

    def tok_of(dx):
        return ((x + dx + NX) % NX) * NC + core

    barrier = pltpu.get_barrier_semaphore()

    def greet(dev):
        pl.semaphore_signal(barrier, inc=1, device_id=dev, device_id_type=MESH)

    greet(at_tok(sib))
    for dx in range(1, NX):
        greet(at_tok(tok_of(dx)))
    for dy in range(1, NY):
        greet(at_out(((y + dy) % NY) * NZ + zh))
    greet(at_out(y * NZ + 1 - zh))
    pl.when(has_up)(lambda: greet(at_inp(zi + 1)))
    pl.when(has_dn)(lambda: greet(at_inp(zi - 1)))
    ends = jnp.where(has_up, 1, 0) + jnp.where(has_dn, 1, 0)
    pl.semaphore_wait(barrier, 1 + (NX - 1) + (NY - 1) + 1 + ends)

    def gather_tok(buf, ss, rs):
        def shard(k):
            return buf.at[pl.ds(pl.multiple_of(k * ts, ts), ts)]

        def copy(k, slot, dev):
            return rc(shard(k), shard(k), ss.at[slot], rs.at[k], dev)

        sends = [copy(t, 0, at_tok(sib))]
        near = []
        if NX > 1:
            near.append(1)
        if NX > 2:
            near.append(-1)
        for i, dx in enumerate(near):
            sends.append(copy(t, 1 + i, at_tok(tok_of(dx))))

        def begin():
            for c in sends:
                c.start()

        def middle():
            slot = 3
            for dx in near:
                k = tok_of(dx)
                copy(k, 0, at_tok(sib)).wait_recv()
                c = copy(k, slot, at_tok(sib))
                c.start()
                sends.append(c)
                slot += 1
            if NX > 2:
                c = copy(tok_of(2 * core - 1), slot, at_tok(tok_of(1 - 2 * core)))
                c.start()
                sends.append(c)

        def end():
            if NX > 2:
                k = tok_of(2)
                copy(k, 0, at_tok(sib)).wait_recv()
                c = copy(k, 6, at_tok(sib))
                c.start()
                sends.append(c)
            for dx in range(NX):
                k = ((x + dx) % NX) * NC + 1 - core
                copy(k, 0, at_tok(sib)).wait_recv()

        def drain():
            for c in sends:
                c.wait_send()

        return begin, middle, end, drain

    def hand(buf, ss, rs, j, up):
        return rc(buf.at[j], buf.at[j], ss.at[up, j], rs.at[j], at_inp(zi + 1 if up else zi - 1))

    def own_both(buf, ss, rs):
        pl.when(has_up)(lambda: hand(buf, ss, rs, zi, 1).start())
        pl.when(has_dn)(lambda: hand(buf, ss, rs, zi, 0).start())

    def pass_on(buf, ss, rs, s):
        @pl.when(zi + s <= NI - 1)
        def _():
            hand(buf, ss, rs, zi + s, 1).wait_recv()
            pl.when(has_dn)(lambda: hand(buf, ss, rs, zi + s, 0).start())

        @pl.when(zi - s >= 0)
        def _():
            hand(buf, ss, rs, zi - s, 0).wait_recv()
            pl.when(has_up)(lambda: hand(buf, ss, rs, zi - s, 1).start())

    def drain_z(buf, ss, rs):
        def body(j, carry):
            pl.when(jnp.logical_and(has_up, j <= zi))(lambda: hand(buf, ss, rs, j, 1).wait_send())
            pl.when(jnp.logical_and(has_dn, j >= zi))(lambda: hand(buf, ss, rs, j, 0).wait_send())
            return carry

        lax.fori_loop(0, NI, body, 0)

    def order(n):
        m = jnp.minimum(zi, NI - 1 - zi)
        half = (n + 1) // 2
        near = jnp.where(n % 2 == 1, zi + half, zi - half)
        far = jnp.where(zi <= m, n, NI - 1 - n)
        return jnp.where(n <= 2 * m, near, far)

    def block(buf, j):
        return buf[pl.ds(pl.multiple_of(j * tb, tb), tb), :]

    def chain(buf, ss, rs, d, up):
        return rc(buf.at[d], buf.at[d], ss.at[d], rs.at[d], at_inp(zi + 1 if up else zi - 1))

    def slot(k):
        @pl.when(jnp.logical_and(zi <= k, has_up))
        def _():
            d = NI - 1 - k + zi
            PS[...] = dot(wd_ref[...], block(GA, d), LAST)

            @pl.when(has_dn)
            def _():
                chain(RU, ru_s, ru_r, d, 1).wait_recv()
                PS[...] += RU[d].astype(F32)

            RU[d] = PS[...].astype(BF16)
            chain(RU, ru_s, ru_r, d, 1).start()

        @pl.when(jnp.logical_and(k >= NI - 1 - zi, has_dn))
        def _():
            d = k - (NI - 1 - zi)
            PS[...] = dot(wd_ref[...], block(GA, d), LAST)

            @pl.when(has_up)
            def _():
                chain(RD, rd_s, rd_r, d, 0).wait_recv()
                PS[...] += RD[d].astype(F32)

            RD[d] = PS[...].astype(BF16)
            chain(RD, rd_s, rd_r, d, 0).start()

    def close_chains():
        PS[...] = dot(wd_ref[...], block(GA, zi), LAST)

        @pl.when(has_dn)
        def _():
            chain(RU, ru_s, ru_r, zi, 1).wait_recv()
            PS[...] += RU[zi].astype(F32)

        @pl.when(has_up)
        def _():
            chain(RD, rd_s, rd_r, zi, 0).wait_recv()
            PS[...] += RD[zi].astype(F32)

        H[zi] = PS[...].astype(BF16)

    def drain_chains():
        def body(d, carry):
            pl.when(jnp.logical_and(has_up, d > zi))(lambda: chain(RU, ru_s, ru_r, d, 1).wait_send())
            pl.when(jnp.logical_and(has_dn, d < zi))(lambda: chain(RD, rd_s, rd_r, d, 0).wait_send())
            return carry

        lax.fori_loop(0, NI, body, 0)

    def terms(n, first):
        j = order(n)
        g, u = GU[j, 0].astype(F32), GU[j, 1].astype(F32)
        sig = 1.0 / (1.0 + jnp.exp(-g))
        gs = g * sig
        TA[n] = u * sig * (1.0 + g * (1.0 - sig))
        TB[n] = gs
        part = dot((gs * u).astype(BF16), block(GA, j))
        if first:
            DW[...] = part
        else:
            DW[...] += part

    def grads(n):
        j = order(n)
        h = H[j].astype(F32)
        gg, ug = (h * TA[n]).astype(BF16), (h * TB[n]).astype(BF16)
        xb = block(XA, j)
        GW[...] += dot(gg, xb)
        UW[...] += dot(ug, xb)
        part = dot(gg, wg_ref[...], LEAD) + dot(ug, wu_ref[...], LEAD)
        part = part.reshape(NX, NC, rows, D)
        for c in range(NC):
            IG2[c, n] = part[:, c]
        ig_core(n).start()

    def ig_core(n):
        return rc(IG2.at[1 - core, n], IGR.at[n], ig_s.at[n], ig_r.at[n], at_tok(sib))

    def ig_x(n, dx):
        return rc(
            XS.at[n, (x + dx) % NX], XR.at[dx - 1, n], xs_s.at[dx - 1, n], xs_r.at[dx - 1, n], at_tok(tok_of(dx))
        )

    def ig_y(dy):
        yd = (y + dy) % NY
        return rc(
            YS.at[pl.ds(yd * NZ, NZ)], YR.at[dy - 1], ys_s.at[dy - 1], ys_r.at[dy - 1], at_out(yd * NZ + zh)
        )

    def sum_core(n):
        ig_core(n).wait()
        XS[n] = IG2[core, n] + IGR[n]
        for dx in range(1, NX):
            ig_x(n, dx).start()

    def sum_x(n):
        total = XS[n, x]
        for dx in range(1, NX):
            ig_x(n, dx).wait()
            total = total + XR[dx - 1, n]
        YS[order(n)] = total

    GA[pl.ds(pl.multiple_of(t * ts, ts), ts), :] = go_ref[...]
    g_begin, g_middle, g_end, g_drain = gather_tok(GA, ga_s, ga_r)
    g_begin()
    GU[zi, 0] = g_ref[...].astype(BF16)
    GU[zi, 1] = u_ref[...].astype(BF16)
    own_both(GU, gu_s, gu_r)
    XA[pl.ds(pl.multiple_of(t * ts, ts), ts), :] = x_ref[...].astype(BF16)
    x_begin, x_middle, x_end, x_drain = gather_tok(XA, xa_s, xa_r)
    g_middle()
    x_begin()
    g_end()
    done_gu = done_terms = 0

    def gu_step():
        nonlocal done_gu
        done_gu += 1
        pass_on(GU, gu_s, gu_r, done_gu)

    def some_terms():
        nonlocal done_terms
        terms(done_terms, done_terms == 0)
        done_terms += 1

    for k in range(NI - 1):
        slot(k)
        want = (k + 1) * 5 // 7
        while done_gu < want:
            gu_step()
        if k == 0:
            x_middle()
        if k == 1:
            x_end()
        if k >= 1 and done_terms <= done_gu:
            some_terms()
    if NI == 2:
        x_end()
    close_chains()
    own_both(H, h_s, h_r)
    while done_gu < NI - 1:
        gu_step()
    while done_terms < NI:
        some_terms()
    GW[...] = jnp.zeros_like(GW)
    UW[...] = jnp.zeros_like(UW)
    grads(0)

    def h_step(s, carry):
        pass_on(H, h_s, h_r, s)
        grads(s)
        sum_core(s - 1)
        pl.when(s >= 2)(lambda: sum_x(s - 2))
        return carry

    lax.fori_loop(1, NI, h_step, 0)
    sum_core(NI - 1)
    sum_x(NI - 2)
    gw_ref[...] = GW[...].astype(BF16)
    uw_ref[...] = UW[...].astype(BF16)
    sum_x(NI - 1)
    for dy in range(1, NY):
        ig_y(dy).start()
    dw_ref[...] = DW[...].astype(BF16)
    total = YS[pl.ds(y * NZ, NZ)]
    for dy in range(1, NY):
        ig_y(dy).wait()
        total = total + YR[dy - 1]
    YS[pl.ds(y * NZ, NZ)] = total
    last = rc(YS.at[y * NZ + 1 - zh], ZR, z_s, z_r, at_out(y * NZ + 1 - zh))
    last.start()
    g_drain()
    x_drain()
    drain_z(GU, gu_s, gu_r)
    drain_z(H, h_s, h_r)
    drain_chains()
    last.wait()
    ig_ref[...] = (YS[o] + ZR[...]).astype(BF16)


def local(saved_input, saved_gate, saved_up, out_grad, w_gate, w_up, w_down):
    sizes = tuple(lax.axis_size(a) for a in ("inp", "out", "tok"))
    NI, NO, NT = sizes
    NX, NY = NT // NC, NO // NZ
    ts, D = saved_input.shape
    tb, F = saved_gate.shape
    T = tb * NI
    rows = tb // NT
    dma = pltpu.SemaphoreType.DMA
    vmem = pl.BlockSpec(memory_space=pltpu.VMEM)
    ig, gw, uw, dw = pl.pallas_call(
        functools.partial(kernel, sizes),
        out_shape=(
            jax.ShapeDtypeStruct((rows, D), BF16),
            jax.ShapeDtypeStruct((F, D), BF16),
            jax.ShapeDtypeStruct((F, D), BF16),
            jax.ShapeDtypeStruct((F, D), BF16),
        ),
        in_specs=[vmem] * 7,
        out_specs=(vmem,) * 4,
        scratch_shapes=[
            pltpu.VMEM((T, D), BF16),
            pltpu.VMEM((T, D), BF16),
            pltpu.VMEM((NI, 2, F, tb), BF16),
            pltpu.VMEM((NI, F, tb), BF16),
            pltpu.VMEM((NI, F, tb), BF16),
            pltpu.VMEM((NI, F, tb), BF16),
            pltpu.VMEM((F, tb), F32),
            pltpu.VMEM((NI, F, tb), F32),
            pltpu.VMEM((NI, F, tb), F32),
            pltpu.VMEM((F, D), F32),
            pltpu.VMEM((F, D), F32),
            pltpu.VMEM((F, D), F32),
            pltpu.VMEM((NC, NI, NX, rows, D), F32),
            pltpu.VMEM((NI, NX, rows, D), F32),
            pltpu.VMEM((NI, NX, rows, D), F32),
            pltpu.VMEM((max(NX - 1, 1), NI, rows, D), F32),
            pltpu.VMEM((NO, rows, D), F32),
            pltpu.VMEM((max(NY - 1, 1), NZ, rows, D), F32),
            pltpu.VMEM((rows, D), F32),
            dma((7,)), dma((NT,)), dma((7,)), dma((NT,)),
            dma((2, NI)), dma((NI,)), dma((2, NI)), dma((NI,)),
            dma((NI,)), dma((NI,)), dma((NI,)), dma((NI,)),
            dma((NI,)), dma((NI,)),
            dma((max(NX - 1, 1), NI)), dma((max(NX - 1, 1), NI)),
            dma((max(NY - 1, 1),)), dma((max(NY - 1, 1),)), dma, dma,
        ],
        compiler_params=pltpu.CompilerParams(
            collective_id=0, has_side_effects=True, vmem_limit_bytes=56 * 1024 * 1024
        ),
    )(saved_input, saved_gate.T, saved_up.T, out_grad, w_gate.T, w_up.T, w_down)
    return ig, gw.T, uw.T, dw


def solution(mesh):
    placed = (
        P("tok", "inp"),
        P("inp", ("out", "tok")),
        P("inp", ("out", "tok")),
        P("tok", "inp"),
        P("inp", ("out", "tok")),
        P("inp", ("out", "tok")),
        P(("out", "tok"), "inp"),
    )
    return jax.shard_map(
        local,
        mesh=mesh,
        in_specs=placed,
        out_specs=(
            P(("out", "tok"), "inp"),
            P("inp", ("out", "tok")),
            P("inp", ("out", "tok")),
            P(("out", "tok"), "inp"),
        ),
        check_vma=False,
    )
```

```python
import functools

import jax
import jax.numpy as jnp
from jax import lax
from jax.experimental import pallas as pl
from jax.experimental.pallas import tpu as pltpu
from jax.sharding import PartitionSpec as P

MESH = pl.DeviceIdType.MESH
F32 = jnp.float32
BF16 = jnp.bfloat16
LAST = (((1,), (1,)), ((), ()))
LEAD = (((0,), (0,)), ((), ()))
NC = 2
NZ = 2
CH = 4
TP = 2
XM, XE = 3, 5
E0 = 3


def dot(a, b, dims=(((1,), (0,)), ((), ()))):
    return lax.dot_general(a, b, dims, preferred_element_type=F32)


def kernel(
    sizes,
    x_in, g_in, u_in, go_in, wg_in, wu_in, wd_in,
    ig_ref, gw_out, uw_out, dw_out,
    XF, GF, UF, WG, WU, WD,
    GA, XA, GU, H, RU, RD, PU, PD, PO, TA, TB, HD, GW, UW, DW, GO, UO, DO, FR,
    IG2, IGR, XS, XB, XR, YS, YR, ZR,
    in_s, out_s, ga_s, ga_r, xa_s, xa_r, gu_s, gu_r, h_s, h_r, ru_s, ru_r, rd_s, rd_r, fr_s, fr_r,
    ig_s, ig_r, xs_s, xs_r, ys_s, ys_r, z_s, z_r,
):
    NI, NO, NT = sizes
    NX, NY = NT // NC, NO // NZ
    zi, o, t = lax.axis_index("inp"), lax.axis_index("out"), lax.axis_index("tok")
    x, core = t // NC, t % NC
    y, zh = o // NZ, o % NZ
    F, tb = g_in.shape
    ts, D = go_in.shape
    fc = F // CH
    rows = tb // NT

    def at_inp(k):
        return {"inp": k}

    def at_tok(k):
        return {"tok": k}

    def at_out(k):
        return {"out": k}

    def rc(src, dst, ss, rs, dev):
        return pltpu.make_async_remote_copy(
            src_ref=src, dst_ref=dst, send_sem=ss, recv_sem=rs, device_id=dev, device_id_type=MESH
        )

    has_up, has_dn = zi < NI - 1, zi > 0
    sib = x * NC + (1 - core)

    def tok_of(dx):
        return ((x + dx + NX) % NX) * NC + core

    def rows_of(buf, k):
        return buf.at[pl.ds(pl.multiple_of(k * ts, ts), ts)]

    loads = [
        pltpu.make_async_copy(src, dst, in_s.at[i])
        for i, (src, dst) in enumerate(
            [(go_in, rows_of(GA, t)), (g_in, GF), (u_in, UF), (x_in, XF), (wd_in, WD), (wg_in, WG), (wu_in, WU)]
        )
    ]
    for c in loads:
        c.start()

    barrier = pltpu.get_barrier_semaphore()

    def greet(dev):
        pl.semaphore_signal(barrier, inc=1, device_id=dev, device_id_type=MESH)

    greet(at_tok(sib))
    for dx in range(1, NX):
        greet(at_tok(tok_of(dx)))
    for dy in range(1, NY):
        greet(at_out(((y + dy) % NY) * NZ + zh))
    greet(at_out(y * NZ + 1 - zh))
    pl.when(has_up)(lambda: greet(at_inp(zi + 1)))
    pl.when(has_dn)(lambda: greet(at_inp(zi - 1)))
    ends = jnp.where(has_up, 1, 0) + jnp.where(has_dn, 1, 0)
    pl.semaphore_wait(barrier, 1 + (NX - 1) + (NY - 1) + 1 + ends)

    def gather_tok(buf, ss, rs, pieces):
        step = ts // pieces

        def copy(k, slot, dev, c):
            part = buf.at[pl.ds(pl.multiple_of(k * ts + c * step, step), step)]
            return rc(part, part, ss.at[slot, c], rs.at[k, c], dev)

        near = [1, -1][: min(NX - 1, 2)]

        def sends():
            yield 0, (t, 0, at_tok(sib))
            for i, dx in enumerate(near):
                yield 0, (t, 1 + i, at_tok(tok_of(dx)))
            for i, dx in enumerate(near):
                yield 1, (tok_of(dx), 3 + i, at_tok(sib))
            if NX > 2:
                yield 1, (tok_of(2 * core - 1), 5, at_tok(tok_of(1 - 2 * core)))
                yield 2, (tok_of(2), 6, at_tok(sib))

        def arrived(k, c):
            copy(k, 0, at_tok(sib), c).wait_recv()

        def start(stage, c):
            for at, args in sends():
                if at == stage:
                    copy(*args, c).start()

        def begin():
            for c in range(pieces):
                start(0, c)

        def middle():
            for c in range(pieces):
                for dx in near:
                    arrived(tok_of(dx), c)
                start(1, c)

        def end():
            for c in range(pieces):
                if NX > 2:
                    arrived(tok_of(2), c)
                    start(2, c)
            for c in range(pieces):
                for dx in range(NX):
                    arrived(((x + dx) % NX) * NC + 1 - core, c)

        def drain():
            for c in range(pieces):
                for _, args in sends():
                    copy(*args, c).wait_send()

        return begin, middle, end, drain

    def hand(buf, ss, rs, j, c, up):
        return rc(buf.at[j, c], buf.at[j, c], ss.at[up, j, c], rs.at[j, c], at_inp(zi + 1 if up else zi - 1))

    def own_both(buf, ss, rs, c):
        pl.when(has_up)(lambda: hand(buf, ss, rs, zi, c, 1).start())
        pl.when(has_dn)(lambda: hand(buf, ss, rs, zi, c, 0).start())

    def pass_on(buf, ss, rs, s, c):
        @pl.when(zi + s <= NI - 1)
        def _():
            hand(buf, ss, rs, zi + s, c, 1).wait_recv()
            pl.when(has_dn)(lambda: hand(buf, ss, rs, zi + s, c, 0).start())

        @pl.when(zi - s >= 0)
        def _():
            hand(buf, ss, rs, zi - s, c, 0).wait_recv()
            pl.when(has_up)(lambda: hand(buf, ss, rs, zi - s, c, 1).start())

    def drain_z(buf, ss, rs, pieces):
        def body(j, carry):
            for c in range(pieces):
                pl.when(jnp.logical_and(has_up, j <= zi))(lambda c=c: hand(buf, ss, rs, j, c, 1).wait_send())
                pl.when(jnp.logical_and(has_dn, j >= zi))(lambda c=c: hand(buf, ss, rs, j, c, 0).wait_send())
            return carry

        lax.fori_loop(0, NI, body, 0)

    def order(n):
        m = jnp.minimum(zi, NI - 1 - zi)
        half = (n + 1) // 2
        near = jnp.where(n % 2 == 1, zi + half, zi - half)
        far = jnp.where(zi <= m, n, NI - 1 - n)
        return jnp.where(n <= 2 * m, near, far)

    def block(buf, j):
        return buf[pl.ds(pl.multiple_of(j * tb, tb), tb), :]

    def chain(buf, ss, rs, d, c, up):
        return rc(buf.at[d, c], buf.at[d, c], ss.at[d, c], rs.at[d, c], at_inp(zi + 1 if up else zi - 1))

    def up_on(k):
        return jnp.logical_and(zi <= k, has_up)

    def dn_on(k):
        return jnp.logical_and(k >= NI - 1 - zi, has_dn)

    def up_dst(k):
        return NI - 1 - k + zi

    def dn_dst(k):
        return k - (NI - 1 - zi)

    def products(k):
        @pl.when(up_on(k))
        def _():
            PU[...] = dot(WD[...], block(GA, up_dst(k)), LAST)

        @pl.when(dn_on(k))
        def _():
            PD[...] = dot(WD[...], block(GA, dn_dst(k)), LAST)

    def slot(k):
        for c in range(CH):
            piece = slice(c * fc, (c + 1) * fc)

            @pl.when(up_on(k))
            def _():
                d = up_dst(k)

                @pl.when(has_dn)
                def _():
                    chain(RU, ru_s, ru_r, d, c, 1).wait_recv()
                    RU[d, c] = (PU[piece, :] + RU[d, c].astype(F32)).astype(BF16)

                @pl.when(jnp.logical_not(has_dn))
                def _():
                    RU[d, c] = PU[piece, :].astype(BF16)

                chain(RU, ru_s, ru_r, d, c, 1).start()

            @pl.when(dn_on(k))
            def _():
                d = dn_dst(k)

                @pl.when(has_up)
                def _():
                    chain(RD, rd_s, rd_r, d, c, 0).wait_recv()
                    RD[d, c] = (PD[piece, :] + RD[d, c].astype(F32)).astype(BF16)

                @pl.when(jnp.logical_not(has_up))
                def _():
                    RD[d, c] = PD[piece, :].astype(BF16)

                chain(RD, rd_s, rd_r, d, c, 0).start()

    def last_hop(c, up):
        src = (PU if up else PD).at[pl.ds(c * fc, fc)]
        return rc(src, FR.at[up, c], fr_s.at[up, c], fr_r.at[up, c], at_inp(zi + 1 if up else zi - 1))

    def last_slot():
        for c in range(CH):
            piece = slice(c * fc, (c + 1) * fc)

            @pl.when(has_up)
            def _():
                @pl.when(has_dn)
                def _():
                    chain(RU, ru_s, ru_r, zi + 1, c, 1).wait_recv()
                    PU[piece, :] += RU[zi + 1, c].astype(F32)

                last_hop(c, 1).start()

            @pl.when(has_dn)
            def _():
                @pl.when(has_up)
                def _():
                    chain(RD, rd_s, rd_r, zi - 1, c, 0).wait_recv()
                    PD[piece, :] += RD[zi - 1, c].astype(F32)

                last_hop(c, 0).start()

    def close_chains(c):
        piece = slice(c * fc, (c + 1) * fc)

        @pl.when(has_dn)
        def _():
            last_hop(c, 1).wait_recv()
            PO[piece, :] += FR[1, c]

        @pl.when(has_up)
        def _():
            last_hop(c, 0).wait_recv()
            PO[piece, :] += FR[0, c]

        H[zi, c] = PO[piece, :].astype(BF16)

    def drain_chains():
        def body(d, carry):
            for c in range(CH):
                pl.when(d > zi + 1)(lambda c=c: chain(RU, ru_s, ru_r, d, c, 1).wait_send())
                pl.when(d < zi - 1)(lambda c=c: chain(RD, rd_s, rd_r, d, c, 0).wait_send())
            return carry

        lax.fori_loop(0, NI, body, 0)
        for c in range(CH):
            pl.when(has_up)(lambda c=c: last_hop(c, 1).wait_send())
            pl.when(has_dn)(lambda c=c: last_hop(c, 0).wait_send())

    def terms(n):
        j = order(n)
        g, u = GU[j, 0].astype(F32), GU[j, 1].astype(F32)
        sig = 1.0 / (1.0 + jnp.exp(-g))
        gs = g * sig
        TA[n] = u * sig * (1.0 + g * (1.0 - sig))
        TB[n] = gs
        HD[n] = (gs * u).astype(BF16)

    def grads(n):
        j = order(n)
        h = H[j].reshape(F, tb).astype(F32)
        gg, ug = (h * TA[n]).astype(BF16), (h * TB[n]).astype(BF16)
        part = dot(gg, WG[...], LEAD) + dot(ug, WU[...], LEAD)
        part = part.reshape(NX, NC, rows, D)
        for c in range(NC):
            IG2[c, n] = part[:, c]
        ig_core(n).start()
        xb = block(XA, j)
        GW[...] += dot(gg, xb)
        UW[...] += dot(ug, xb)
        DW[...] += dot(HD[n], block(GA, j))

    def ig_core(n):
        return rc(IG2.at[1 - core, n], IGR.at[n], ig_s.at[n], ig_r.at[n], at_tok(sib))

    def ig_x(n, dx):
        return rc(
            XB.at[n, (x + dx) % NX], XR.at[dx - 1, n], xs_s.at[dx - 1, n], xs_r.at[dx - 1, n], at_tok(tok_of(dx))
        )

    def ig_y(n):
        j = order(n)
        root = j // NZ
        far = (y - root + NY) % NY - 1
        return rc(YS.at[j], YR.at[far, j % NZ], ys_s.at[n], ys_r.at[far, j % NZ], at_out(root * NZ + zh))

    def ig_z():
        j = y * NZ + 1 - zh
        return rc(YS.at[j], ZR, z_s, z_r, at_out(j))

    def sum_core(n):
        ig_core(n).wait()
        XS[n] = IG2[core, n] + IGR[n]
        XB[n] = XS[n].astype(BF16)
        for dx in range(1, NX):
            ig_x(n, dx).start()

    def sum_x(n):
        total = XS[n, x]
        for dx in range(1, NX):
            ig_x(n, dx).wait()
            total = total + XR[dx - 1, n].astype(F32)
        YS[order(n)] = total
        pl.when(y != order(n) // NZ)(lambda: ig_y(n).start())

    def sum_y(n):
        j = order(n)

        @pl.when(y != j // NZ)
        def _():
            ig_y(n).wait_send()

        @pl.when(y == j // NZ)
        def _():
            total = YS[j]
            for far in range(NY - 1):
                rc(YS.at[j], YR.at[far, j % NZ], ys_s.at[n], ys_r.at[far, j % NZ], at_out(y * NZ + 1 - zh)).wait_recv()
                total = total + YR[far, j % NZ]
            YS[j] = total
            pl.when(zh != j % NZ)(lambda: ig_z().start())

    loads[0].wait()
    g_begin, g_middle, g_end, g_drain = gather_tok(GA, ga_s, ga_r, TP)
    g_begin()
    loads[1].wait()
    GU[zi, 0] = GF[...].astype(BF16)
    own_both(GU, gu_s, gu_r, 0)
    loads[2].wait()
    GU[zi, 1] = UF[...].astype(BF16)
    own_both(GU, gu_s, gu_r, 1)
    loads[3].wait()
    XA[pl.ds(pl.multiple_of(t * ts, ts), ts), :] = XF[...].astype(BF16)
    x_begin, x_middle, x_end, x_drain = gather_tok(XA, xa_s, xa_r, TP)

    def gu_event(e):
        pl.when(e < 2 * (NI - 1))(lambda: pass_on(GU, gu_s, gu_r, e // 2 + 1, e % 2))

    GW[...] = jnp.zeros_like(GW)
    UW[...] = jnp.zeros_like(UW)
    DW[...] = jnp.zeros_like(DW)
    for c in loads[4:]:
        c.wait()
    g_middle()
    x_begin()
    for e in range(E0):
        gu_event(e)
    g_end()
    products(0)

    def rs_step(k, carry):
        slot(k)
        gu_event(E0 + k)
        products(k + 1)
        pl.when(k == XM)(x_middle)
        pl.when(k == XE)(x_end)
        pl.when(k >= 2)(lambda: terms(k - 2))
        return carry

    lax.fori_loop(0, NI - 2, rs_step, 0)
    last_slot()
    gu_event(E0 + NI - 2)
    if XM > NI - 3:
        x_middle()
    if XE > NI - 3:
        x_end()
    first_terms = max(NI - 4, 0)
    PO[...] = dot(WD[...], block(GA, zi), LAST)
    for c in range(CH):
        close_chains(c)
        own_both(H, h_s, h_r, c)
    events = E0 + NI - 1

    def h_step(s, carry):
        for c in range(CH):
            pass_on(H, h_s, h_r, s, c)
            if c == 0:
                gu_event(events + s - 1)
        for n in range(first_terms, NI):
            pl.when(s == max(n - first_terms, 2 * n - events, 1))(lambda n=n: terms(n))
        pl.when(s == 1)(lambda: grads(0))
        grads(s)
        sum_core(s - 1)
        pl.when(s >= 2)(lambda: sum_x(s - 2))
        pl.when(s >= 3)(lambda: sum_y(s - 3))
        return carry

    lax.fori_loop(1, NI, h_step, 0)
    sum_core(NI - 1)
    outs = []
    for i, (acc, stage, out) in enumerate([(GW, GO, gw_out), (UW, UO, uw_out), (DW, DO, dw_out)]):
        if i == 1:
            sum_x(NI - 2)
            sum_x(NI - 1)
        stage[...] = acc[...].astype(BF16)
        outs.append(pltpu.make_async_copy(stage, out, out_s.at[i]))
        outs[-1].start()
    for n in range(max(NI - 3, 0), NI):
        sum_y(n)
    g_drain()
    x_drain()
    drain_z(GU, gu_s, gu_r, 2)
    drain_z(H, h_s, h_r, CH)
    drain_chains()
    ig_z().wait()
    ig_ref[...] = (YS[o] + ZR[...]).astype(BF16)
    for c in outs:
        c.wait()


def copy_out(*refs):
    n = (len(refs) - 2) // 3
    ins, outs, held, (in_s, out_s) = refs[:n], refs[n : 2 * n], refs[2 * n : 3 * n], refs[3 * n :]
    first = [pltpu.make_async_copy(ins[i], held[i], in_s.at[i]) for i in range(n)]
    second = [pltpu.make_async_copy(held[i], outs[i], out_s.at[i]) for i in range(n)]
    for c in first:
        c.start()
    for c, d in zip(first, second):
        c.wait()
        d.start()
    for d in second:
        d.wait()


def local(saved_input, saved_gate, saved_up, out_grad, w_gate, w_up, w_down):
    sizes = tuple(lax.axis_size(a) for a in ("inp", "out", "tok"))
    NI, NO, NT = sizes
    NX, NY = NT // NC, NO // NZ
    ts, D = saved_input.shape
    tb, F = saved_gate.shape
    T = tb * NI
    rows = tb // NT
    dma = pltpu.SemaphoreType.DMA
    vmem = pl.BlockSpec(memory_space=pltpu.VMEM)
    anyw = pl.BlockSpec(memory_space=pl.ANY)
    fc = F // CH
    ig, gw, uw, dw = pl.pallas_call(
        functools.partial(kernel, sizes),
        out_shape=(
            jax.ShapeDtypeStruct((rows, D), BF16),
            jax.ShapeDtypeStruct((F, D), BF16),
            jax.ShapeDtypeStruct((F, D), BF16),
            jax.ShapeDtypeStruct((F, D), BF16),
        ),
        in_specs=[anyw] * 7,
        out_specs=(vmem, anyw, anyw, anyw),
        scratch_shapes=[
            pltpu.VMEM((ts, D), F32),
            pltpu.VMEM((F, tb), F32),
            pltpu.VMEM((F, tb), F32),
            pltpu.VMEM((F, D), BF16),
            pltpu.VMEM((F, D), BF16),
            pltpu.VMEM((F, D), BF16),
            pltpu.VMEM((T, D), BF16),
            pltpu.VMEM((T, D), BF16),
            pltpu.VMEM((NI, 2, F, tb), BF16),
            pltpu.VMEM((NI, CH, fc, tb), BF16),
            pltpu.VMEM((NI, CH, fc, tb), BF16),
            pltpu.VMEM((NI, CH, fc, tb), BF16),
            pltpu.VMEM((F, tb), F32),
            pltpu.VMEM((F, tb), F32),
            pltpu.VMEM((F, tb), F32),
            pltpu.VMEM((NI, F, tb), F32),
            pltpu.VMEM((NI, F, tb), F32),
            pltpu.VMEM((NI, F, tb), BF16),
            pltpu.VMEM((F, D), F32),
            pltpu.VMEM((F, D), F32),
            pltpu.VMEM((F, D), F32),
            pltpu.VMEM((F, D), BF16),
            pltpu.VMEM((F, D), BF16),
            pltpu.VMEM((F, D), BF16),
            pltpu.VMEM((2, CH, fc, tb), F32),
            pltpu.VMEM((NC, NI, NX, rows, D), F32),
            pltpu.VMEM((NI, NX, rows, D), F32),
            pltpu.VMEM((NI, NX, rows, D), F32),
            pltpu.VMEM((NI, NX, rows, D), BF16),
            pltpu.VMEM((max(NX - 1, 1), NI, rows, D), BF16),
            pltpu.VMEM((NO, rows, D), F32),
            pltpu.VMEM((max(NY - 1, 1), NZ, rows, D), F32),
            pltpu.VMEM((rows, D), F32),
            dma((7,)), dma((3,)),
            dma((7, TP)), dma((NT, TP)), dma((7, TP)), dma((NT, TP)),
            dma((2, NI, 2)), dma((NI, 2)), dma((2, NI, CH)), dma((NI, CH)),
            dma((NI, CH)), dma((NI, CH)), dma((NI, CH)), dma((NI, CH)), dma((2, CH)), dma((2, CH)),
            dma((NI,)), dma((NI,)),
            dma((max(NX - 1, 1), NI)), dma((max(NX - 1, 1), NI)),
            dma((NI,)), dma((max(NY - 1, 1), NZ)), dma, dma,
        ],
        compiler_params=pltpu.CompilerParams(
            collective_id=0, has_side_effects=True, vmem_limit_bytes=56 * 1024 * 1024
        ),
    )(saved_input, saved_gate.T, saved_up.T, out_grad, w_gate.T, w_up.T, w_down)
    results = (ig, gw, uw, dw)
    ig, gw, uw, dw = pl.pallas_call(
        copy_out,
        out_shape=tuple(jax.ShapeDtypeStruct(r.shape, r.dtype) for r in results),
        in_specs=[anyw] * 4,
        out_specs=(anyw,) * 4,
        scratch_shapes=[pltpu.VMEM(r.shape, r.dtype) for r in results] + [dma((4,)), dma((4,))],
    )(*results)
    return ig, gw.T, uw.T, dw


def solution(mesh):
    placed = (
        P("tok", "inp"),
        P("inp", ("out", "tok")),
        P("inp", ("out", "tok")),
        P("tok", "inp"),
        P("inp", ("out", "tok")),
        P("inp", ("out", "tok")),
        P(("out", "tok"), "inp"),
    )
    return jax.shard_map(
        local,
        mesh=mesh,
        in_specs=placed,
        out_specs=(
            P(("out", "tok"), "inp"),
            P("inp", ("out", "tok")),
            P("inp", ("out", "tok")),
            P(("out", "tok"), "inp"),
        ),
        check_vma=False,
    )
```

```python
import functools

import jax
import jax.numpy as jnp
from jax import lax
from jax.experimental import pallas as pl
from jax.experimental.pallas import tpu as pltpu
from jax.sharding import PartitionSpec as P

MESH = pl.DeviceIdType.MESH
F32 = jnp.float32
BF16 = jnp.bfloat16
LAST = (((1,), (1,)), ((), ()))
LEAD = (((0,), (0,)), ((), ()))
NC = 2
NZ = 2
CH = 4
TP = 2
XM, XE = 3, 5
LAST_HOP = BF16
Z_HOP = BF16
E0 = 3


def dot(a, b, dims=(((1,), (0,)), ((), ()))):
    return lax.dot_general(a, b, dims, preferred_element_type=F32)


def kernel(
    sizes,
    x_in, g_in, u_in, go_in, wg_in, wu_in, wd_in,
    ig_ref, gw_out, uw_out, dw_out,
    XF, GF, UF, WG, WU, WD,
    GA, XA, GU, H, RU, RD, PU, PD, PO, TA, TB, HD, GW, UW, DW, FS, FR,
    IG2, IGR, XS, XB, XR, YS, YR, ZS, ZR,
    in_s, ga_s, ga_r, xa_s, xa_r, gu_s, gu_r, h_s, h_r, ru_s, ru_r, rd_s, rd_r, fr_s, fr_r,
    ig_s, ig_r, xs_s, xs_r, ys_s, ys_r, z_s, z_r,
):
    NI, NO, NT = sizes
    NX, NY = NT // NC, NO // NZ
    zi, o, t = lax.axis_index("inp"), lax.axis_index("out"), lax.axis_index("tok")
    x, core = t // NC, t % NC
    y, zh = o // NZ, o % NZ
    F, tb = g_in.shape
    ts, D = go_in.shape
    fc = F // CH
    rows = tb // NT

    def at_inp(k):
        return {"inp": k}

    def at_tok(k):
        return {"tok": k}

    def at_out(k):
        return {"out": k}

    def rc(src, dst, ss, rs, dev):
        return pltpu.make_async_remote_copy(
            src_ref=src, dst_ref=dst, send_sem=ss, recv_sem=rs, device_id=dev, device_id_type=MESH
        )

    has_up, has_dn = zi < NI - 1, zi > 0
    sib = x * NC + (1 - core)

    def tok_of(dx):
        return ((x + dx + NX) % NX) * NC + core

    def rows_of(buf, k):
        return buf.at[pl.ds(pl.multiple_of(k * ts, ts), ts)]

    loads = [
        pltpu.make_async_copy(src, dst, in_s.at[i])
        for i, (src, dst) in enumerate(
            [(go_in, rows_of(GA, t)), (g_in, GF), (u_in, UF), (x_in, XF), (wd_in, WD), (wg_in, WG), (wu_in, WU)]
        )
    ]
    for c in loads:
        c.start()

    barrier = pltpu.get_barrier_semaphore()

    def greet(dev):
        pl.semaphore_signal(barrier, inc=1, device_id=dev, device_id_type=MESH)

    greet(at_tok(sib))
    for dx in range(1, NX):
        greet(at_tok(tok_of(dx)))
    for dy in range(1, NY):
        greet(at_out(((y + dy) % NY) * NZ + zh))
    greet(at_out(y * NZ + 1 - zh))
    pl.when(has_up)(lambda: greet(at_inp(zi + 1)))
    pl.when(has_dn)(lambda: greet(at_inp(zi - 1)))
    ends = jnp.where(has_up, 1, 0) + jnp.where(has_dn, 1, 0)
    pl.semaphore_wait(barrier, 1 + (NX - 1) + (NY - 1) + 1 + ends)

    def gather_tok(buf, ss, rs, pieces):
        step = ts // pieces

        def copy(k, slot, dev, c):
            part = buf.at[pl.ds(pl.multiple_of(k * ts + c * step, step), step)]
            return rc(part, part, ss.at[slot, c], rs.at[k, c], dev)

        near = [1, -1][: min(NX - 1, 2)]

        def sends():
            yield 0, (t, 0, at_tok(sib))
            for i, dx in enumerate(near):
                yield 0, (t, 1 + i, at_tok(tok_of(dx)))
            for i, dx in enumerate(near):
                yield 1, (tok_of(dx), 3 + i, at_tok(sib))
            if NX > 2:
                yield 1, (tok_of(2 * core - 1), 5, at_tok(tok_of(1 - 2 * core)))
                yield 2, (tok_of(2), 6, at_tok(sib))

        def arrived(k, c):
            copy(k, 0, at_tok(sib), c).wait_recv()

        def start(stage, c):
            for at, args in sends():
                if at == stage:
                    copy(*args, c).start()

        def begin():
            for c in range(pieces):
                start(0, c)

        def middle():
            for c in range(pieces):
                for dx in near:
                    arrived(tok_of(dx), c)
                start(1, c)

        def end():
            for c in range(pieces):
                if NX > 2:
                    arrived(tok_of(2), c)
                    start(2, c)
            for c in range(pieces):
                for dx in range(NX):
                    arrived(((x + dx) % NX) * NC + 1 - core, c)

        def drain():
            for c in range(pieces):
                for _, args in sends():
                    copy(*args, c).wait_send()

        return begin, middle, end, drain

    def hand(buf, ss, rs, j, c, up):
        return rc(buf.at[j, c], buf.at[j, c], ss.at[up, j, c], rs.at[j, c], at_inp(zi + 1 if up else zi - 1))

    def own_both(buf, ss, rs, c):
        pl.when(has_up)(lambda: hand(buf, ss, rs, zi, c, 1).start())
        pl.when(has_dn)(lambda: hand(buf, ss, rs, zi, c, 0).start())

    def pass_on(buf, ss, rs, s, c):
        @pl.when(zi + s <= NI - 1)
        def _():
            hand(buf, ss, rs, zi + s, c, 1).wait_recv()
            pl.when(has_dn)(lambda: hand(buf, ss, rs, zi + s, c, 0).start())

        @pl.when(zi - s >= 0)
        def _():
            hand(buf, ss, rs, zi - s, c, 0).wait_recv()
            pl.when(has_up)(lambda: hand(buf, ss, rs, zi - s, c, 1).start())

    def drain_z(buf, ss, rs, pieces):
        def body(j, carry):
            for c in range(pieces):
                pl.when(jnp.logical_and(has_up, j <= zi))(lambda c=c: hand(buf, ss, rs, j, c, 1).wait_send())
                pl.when(jnp.logical_and(has_dn, j >= zi))(lambda c=c: hand(buf, ss, rs, j, c, 0).wait_send())
            return carry

        lax.fori_loop(0, NI, body, 0)

    def order(n):
        m = jnp.minimum(zi, NI - 1 - zi)
        half = (n + 1) // 2
        near = jnp.where(n % 2 == 1, zi + half, zi - half)
        far = jnp.where(zi <= m, n, NI - 1 - n)
        return jnp.where(n <= 2 * m, near, far)

    def block(buf, j):
        return buf[pl.ds(pl.multiple_of(j * tb, tb), tb), :]

    def chain(buf, ss, rs, d, c, up):
        return rc(buf.at[d, c], buf.at[d, c], ss.at[d, c], rs.at[d, c], at_inp(zi + 1 if up else zi - 1))

    def up_on(k):
        return jnp.logical_and(zi <= k, has_up)

    def dn_on(k):
        return jnp.logical_and(k >= NI - 1 - zi, has_dn)

    def up_dst(k):
        return NI - 1 - k + zi

    def dn_dst(k):
        return k - (NI - 1 - zi)

    def products(k):
        @pl.when(up_on(k))
        def _():
            PU[...] = dot(WD[...], block(GA, up_dst(k)), LAST)

        @pl.when(dn_on(k))
        def _():
            PD[...] = dot(WD[...], block(GA, dn_dst(k)), LAST)

    def slot(k):
        for c in range(CH):
            piece = slice(c * fc, (c + 1) * fc)

            @pl.when(up_on(k))
            def _():
                d = up_dst(k)

                @pl.when(has_dn)
                def _():
                    chain(RU, ru_s, ru_r, d, c, 1).wait_recv()
                    RU[d, c] = (PU[piece, :] + RU[d, c].astype(F32)).astype(BF16)

                @pl.when(jnp.logical_not(has_dn))
                def _():
                    RU[d, c] = PU[piece, :].astype(BF16)

                chain(RU, ru_s, ru_r, d, c, 1).start()

            @pl.when(dn_on(k))
            def _():
                d = dn_dst(k)

                @pl.when(has_up)
                def _():
                    chain(RD, rd_s, rd_r, d, c, 0).wait_recv()
                    RD[d, c] = (PD[piece, :] + RD[d, c].astype(F32)).astype(BF16)

                @pl.when(jnp.logical_not(has_up))
                def _():
                    RD[d, c] = PD[piece, :].astype(BF16)

                chain(RD, rd_s, rd_r, d, c, 0).start()

    def last_hop(c, up):
        return rc(FS.at[up, c], FR.at[up, c], fr_s.at[up, c], fr_r.at[up, c], at_inp(zi + 1 if up else zi - 1))

    def last_slot():
        for c in range(CH):
            piece = slice(c * fc, (c + 1) * fc)

            @pl.when(has_up)
            def _():
                @pl.when(has_dn)
                def _():
                    chain(RU, ru_s, ru_r, zi + 1, c, 1).wait_recv()
                    PU[piece, :] += RU[zi + 1, c].astype(F32)

                FS[1, c] = PU[piece, :].astype(FS.dtype)
                last_hop(c, 1).start()

            @pl.when(has_dn)
            def _():
                @pl.when(has_up)
                def _():
                    chain(RD, rd_s, rd_r, zi - 1, c, 0).wait_recv()
                    PD[piece, :] += RD[zi - 1, c].astype(F32)

                FS[0, c] = PD[piece, :].astype(FS.dtype)
                last_hop(c, 0).start()

    def close_chains(c):
        piece = slice(c * fc, (c + 1) * fc)

        @pl.when(has_dn)
        def _():
            last_hop(c, 1).wait_recv()
            PO[piece, :] += FR[1, c].astype(F32)

        @pl.when(has_up)
        def _():
            last_hop(c, 0).wait_recv()
            PO[piece, :] += FR[0, c].astype(F32)

        H[zi, c] = PO[piece, :].astype(BF16)

    def drain_chains():
        def body(d, carry):
            for c in range(CH):
                pl.when(d > zi + 1)(lambda c=c: chain(RU, ru_s, ru_r, d, c, 1).wait_send())
                pl.when(d < zi - 1)(lambda c=c: chain(RD, rd_s, rd_r, d, c, 0).wait_send())
            return carry

        lax.fori_loop(0, NI, body, 0)
        for c in range(CH):
            pl.when(has_up)(lambda c=c: last_hop(c, 1).wait_send())
            pl.when(has_dn)(lambda c=c: last_hop(c, 0).wait_send())

    def terms(n):
        j = order(n)
        g, u = GU[j, 0].astype(F32), GU[j, 1].astype(F32)
        sig = 1.0 / (1.0 + jnp.exp(-g))
        gs = g * sig
        TA[n] = u * sig * (1.0 + g * (1.0 - sig))
        TB[n] = gs
        HD[n] = (gs * u).astype(BF16)

    def grads(n):
        j = order(n)
        h = H[j].reshape(F, tb).astype(F32)
        gg, ug = (h * TA[n]).astype(BF16), (h * TB[n]).astype(BF16)
        part = dot(gg, WG[...], LEAD) + dot(ug, WU[...], LEAD)
        part = part.reshape(NX, NC, rows, D)
        for c in range(NC):
            IG2[c, n] = part[:, c]
        ig_core(n).start()
        xb = block(XA, j)
        GW[...] += dot(gg, xb)
        UW[...] += dot(ug, xb)
        DW[...] += dot(HD[n], block(GA, j))

    def ig_core(n):
        return rc(IG2.at[1 - core, n], IGR.at[n], ig_s.at[n], ig_r.at[n], at_tok(sib))

    def ig_x(n, dx):
        return rc(
            XB.at[n, (x + dx) % NX], XR.at[dx - 1, n], xs_s.at[dx - 1, n], xs_r.at[dx - 1, n], at_tok(tok_of(dx))
        )

    def ig_y(n):
        j = order(n)
        root = j // NZ
        far = (y - root + NY) % NY - 1
        return rc(YS.at[j], YR.at[far, j % NZ], ys_s.at[n], ys_r.at[far, j % NZ], at_out(root * NZ + zh))

    def ig_z():
        j = y * NZ + 1 - zh
        return rc(ZS, ZR, z_s, z_r, at_out(j))

    def sum_core(n):
        ig_core(n).wait()
        XS[n] = IG2[core, n] + IGR[n]
        XB[n] = XS[n].astype(BF16)
        for dx in range(1, NX):
            ig_x(n, dx).start()

    def sum_x(n):
        total = XS[n, x]
        for dx in range(1, NX):
            ig_x(n, dx).wait()
            total = total + XR[dx - 1, n].astype(F32)
        YS[order(n)] = total
        pl.when(y != order(n) // NZ)(lambda: ig_y(n).start())

    def sum_y(n):
        j = order(n)

        @pl.when(y != j // NZ)
        def _():
            ig_y(n).wait_send()

        @pl.when(y == j // NZ)
        def _():
            total = YS[j]
            for far in range(NY - 1):
                rc(YS.at[j], YR.at[far, j % NZ], ys_s.at[n], ys_r.at[far, j % NZ], at_out(y * NZ + 1 - zh)).wait_recv()
                total = total + YR[far, j % NZ]
            YS[j] = total

            @pl.when(zh != j % NZ)
            def _():
                ZS[...] = total.astype(ZS.dtype)
                ig_z().start()

    loads[0].wait()
    g_begin, g_middle, g_end, g_drain = gather_tok(GA, ga_s, ga_r, TP)
    g_begin()
    loads[1].wait()
    GU[zi, 0] = GF[...].astype(BF16)
    own_both(GU, gu_s, gu_r, 0)
    loads[2].wait()
    GU[zi, 1] = UF[...].astype(BF16)
    own_both(GU, gu_s, gu_r, 1)
    loads[3].wait()
    XA[pl.ds(pl.multiple_of(t * ts, ts), ts), :] = XF[...].astype(BF16)
    x_begin, x_middle, x_end, x_drain = gather_tok(XA, xa_s, xa_r, TP)

    def gu_event(e):
        pl.when(e < 2 * (NI - 1))(lambda: pass_on(GU, gu_s, gu_r, e // 2 + 1, e % 2))

    GW[...] = jnp.zeros_like(GW)
    UW[...] = jnp.zeros_like(UW)
    DW[...] = jnp.zeros_like(DW)
    for c in loads[4:]:
        c.wait()
    g_middle()
    x_begin()
    for e in range(E0):
        gu_event(e)
    g_end()
    products(0)

    def rs_step(k, carry):
        slot(k)
        gu_event(E0 + k)
        products(k + 1)
        pl.when(k == XM)(x_middle)
        pl.when(k == XE)(x_end)
        pl.when(k >= 2)(lambda: terms(k - 2))
        return carry

    lax.fori_loop(0, NI - 2, rs_step, 0)
    last_slot()
    gu_event(E0 + NI - 2)
    if XM > NI - 3:
        x_middle()
    if XE > NI - 3:
        x_end()
    first_terms = max(NI - 4, 0)
    PO[...] = dot(WD[...], block(GA, zi), LAST)
    for c in range(CH):
        close_chains(c)
        own_both(H, h_s, h_r, c)
    events = E0 + NI - 1

    def h_step(s, carry):
        for c in range(CH):
            pass_on(H, h_s, h_r, s, c)
            if c == 0:
                gu_event(events + s - 1)
        for n in range(first_terms, NI):
            pl.when(s == max(n - first_terms, 2 * n - events, 1))(lambda n=n: terms(n))
        pl.when(s == 1)(lambda: grads(0))
        grads(s)
        sum_core(s - 1)
        pl.when(s >= 2)(lambda: sum_x(s - 2))
        pl.when(s >= 3)(lambda: sum_y(s - 3))
        return carry

    lax.fori_loop(1, NI, h_step, 0)
    sum_core(NI - 1)
    gw_out[...] = GW[...].astype(BF16)
    sum_x(NI - 2)
    sum_x(NI - 1)
    uw_out[...] = UW[...].astype(BF16)
    for n in range(max(NI - 3, 0), NI):
        sum_y(n)
    dw_out[...] = DW[...].astype(BF16)
    g_drain()
    x_drain()
    drain_z(GU, gu_s, gu_r, 2)
    drain_z(H, h_s, h_r, CH)
    drain_chains()
    ig_z().wait()
    ig_ref[...] = (YS[o] + ZR[...].astype(F32)).astype(BF16)


def copy_out(*refs):
    n = len(refs) // 2
    copies = [pltpu.make_async_copy(refs[i], refs[n + i], refs[-1].at[i]) for i in range(n)]
    for c in copies:
        c.start()
    for c in copies:
        c.wait()


def local(saved_input, saved_gate, saved_up, out_grad, w_gate, w_up, w_down):
    sizes = tuple(lax.axis_size(a) for a in ("inp", "out", "tok"))
    NI, NO, NT = sizes
    NX, NY = NT // NC, NO // NZ
    ts, D = saved_input.shape
    tb, F = saved_gate.shape
    T = tb * NI
    rows = tb // NT
    dma = pltpu.SemaphoreType.DMA
    vmem = pl.BlockSpec(memory_space=pltpu.VMEM)
    anyw = pl.BlockSpec(memory_space=pl.ANY)
    fc = F // CH
    ig, gw, uw, dw = pl.pallas_call(
        functools.partial(kernel, sizes),
        out_shape=(
            pltpu.VMEM((rows, D), BF16),
            pltpu.VMEM((F, D), BF16),
            pltpu.VMEM((F, D), BF16),
            pltpu.VMEM((F, D), BF16),
        ),
        in_specs=[anyw] * 7,
        out_specs=(vmem,) * 4,
        scratch_shapes=[
            pltpu.VMEM((ts, D), F32),
            pltpu.VMEM((F, tb), F32),
            pltpu.VMEM((F, tb), F32),
            pltpu.VMEM((F, D), BF16),
            pltpu.VMEM((F, D), BF16),
            pltpu.VMEM((F, D), BF16),
            pltpu.VMEM((T, D), BF16),
            pltpu.VMEM((T, D), BF16),
            pltpu.VMEM((NI, 2, F, tb), BF16),
            pltpu.VMEM((NI, CH, fc, tb), BF16),
            pltpu.VMEM((NI, CH, fc, tb), BF16),
            pltpu.VMEM((NI, CH, fc, tb), BF16),
            pltpu.VMEM((F, tb), F32),
            pltpu.VMEM((F, tb), F32),
            pltpu.VMEM((F, tb), F32),
            pltpu.VMEM((NI, F, tb), F32),
            pltpu.VMEM((NI, F, tb), F32),
            pltpu.VMEM((NI, F, tb), BF16),
            pltpu.VMEM((F, D), F32),
            pltpu.VMEM((F, D), F32),
            pltpu.VMEM((F, D), F32),
            pltpu.VMEM((2, CH, fc, tb), LAST_HOP),
            pltpu.VMEM((2, CH, fc, tb), LAST_HOP),
            pltpu.VMEM((NC, NI, NX, rows, D), F32),
            pltpu.VMEM((NI, NX, rows, D), F32),
            pltpu.VMEM((NI, NX, rows, D), F32),
            pltpu.VMEM((NI, NX, rows, D), BF16),
            pltpu.VMEM((max(NX - 1, 1), NI, rows, D), BF16),
            pltpu.VMEM((NO, rows, D), F32),
            pltpu.VMEM((max(NY - 1, 1), NZ, rows, D), F32),
            pltpu.VMEM((rows, D), Z_HOP),
            pltpu.VMEM((rows, D), Z_HOP),
            dma((7,)),
            dma((7, TP)), dma((NT, TP)), dma((7, TP)), dma((NT, TP)),
            dma((2, NI, 2)), dma((NI, 2)), dma((2, NI, CH)), dma((NI, CH)),
            dma((NI, CH)), dma((NI, CH)), dma((NI, CH)), dma((NI, CH)), dma((2, CH)), dma((2, CH)),
            dma((NI,)), dma((NI,)),
            dma((max(NX - 1, 1), NI)), dma((max(NX - 1, 1), NI)),
            dma((NI,)), dma((max(NY - 1, 1), NZ)), dma, dma,
        ],
        compiler_params=pltpu.CompilerParams(
            collective_id=0, has_side_effects=True, vmem_limit_bytes=56 * 1024 * 1024
        ),
    )(saved_input, saved_gate.T, saved_up.T, out_grad, w_gate.T, w_up.T, w_down)
    results = (ig, gw, uw, dw)
    ig, gw, uw, dw = pl.pallas_call(
        copy_out,
        out_shape=tuple(jax.ShapeDtypeStruct(r.shape, r.dtype) for r in results),
        in_specs=[vmem] * 4,
        out_specs=(anyw,) * 4,
        scratch_shapes=[dma((4,))],
    )(*[pltpu.with_memory_space_constraint(r, pltpu.VMEM) for r in results])
    return ig, gw.T, uw.T, dw


def solution(mesh):
    placed = (
        P("tok", "inp"),
        P("inp", ("out", "tok")),
        P("inp", ("out", "tok")),
        P("tok", "inp"),
        P("inp", ("out", "tok")),
        P("inp", ("out", "tok")),
        P(("out", "tok"), "inp"),
    )
    return jax.shard_map(
        local,
        mesh=mesh,
        in_specs=placed,
        out_specs=(
            P(("out", "tok"), "inp"),
            P("inp", ("out", "tok")),
            P("inp", ("out", "tok")),
            P(("out", "tok"), "inp"),
        ),
        check_vma=False,
    )
```

```python
import functools

import jax
import jax.numpy as jnp
from jax import lax
from jax.experimental import pallas as pl
from jax.experimental.pallas import tpu as pltpu
from jax.sharding import PartitionSpec as P

MESH = pl.DeviceIdType.MESH
F32 = jnp.float32
BF16 = jnp.bfloat16
LAST = (((1,), (1,)), ((), ()))
LEAD = (((0,), (0,)), ((), ()))
NC = 2
NZ = 2
CH = 4
TP = 1
XM, XE = 3, 5
LAST_HOP = BF16
Z_HOP = F32
E0 = 4


def dot(a, b, dims=(((1,), (0,)), ((), ()))):
    return lax.dot_general(a, b, dims, preferred_element_type=F32)


def kernel(
    sizes,
    x_in, g_in, u_in, go_in, wg_in, wu_in, wd_in,
    ig_ref, gw_out, uw_out, dw_out,
    XF, GF, UF, WG, WU, WD,
    GA, XA, GU, H, RU, RD, PU, PD, PO, TA, TB, HD, GW, UW, DW, FS, FR,
    IG2, IGR, XS, XB, XR, YS, YR, ZS, ZR,
    in_s, ga_s, ga_r, xa_s, xa_r, gu_s, gu_r, h_s, h_r, ru_s, ru_r, rd_s, rd_r, fr_s, fr_r,
    ig_s, ig_r, xs_s, xs_r, ys_s, ys_r, z_s, z_r,
):
    NI, NO, NT = sizes
    NX, NY = NT // NC, NO // NZ
    zi, o, t = lax.axis_index("inp"), lax.axis_index("out"), lax.axis_index("tok")
    x, core = t // NC, t % NC
    y, zh = o // NZ, o % NZ
    F, tb = g_in.shape
    ts, D = go_in.shape
    fc = F // CH
    rows = tb // NT

    def at_inp(k):
        return {"inp": k}

    def at_tok(k):
        return {"tok": k}

    def at_out(k):
        return {"out": k}

    def rc(src, dst, ss, rs, dev):
        return pltpu.make_async_remote_copy(
            src_ref=src, dst_ref=dst, send_sem=ss, recv_sem=rs, device_id=dev, device_id_type=MESH
        )

    has_up, has_dn = zi < NI - 1, zi > 0
    sib = x * NC + (1 - core)

    def tok_of(dx):
        return ((x + dx + NX) % NX) * NC + core

    def rows_of(buf, k):
        return buf.at[pl.ds(pl.multiple_of(k * ts, ts), ts)]

    loads = [
        pltpu.make_async_copy(src, dst, in_s.at[i])
        for i, (src, dst) in enumerate(
            [(go_in, rows_of(GA, t)), (g_in, GF), (u_in, UF), (x_in, XF), (wd_in, WD), (wg_in, WG), (wu_in, WU)]
        )
    ]
    for c in loads:
        c.start()

    barrier = pltpu.get_barrier_semaphore()

    def greet(dev):
        pl.semaphore_signal(barrier, inc=1, device_id=dev, device_id_type=MESH)

    greet(at_tok(sib))
    for dx in range(1, NX):
        greet(at_tok(tok_of(dx)))
    for dy in range(1, NY):
        greet(at_out(((y + dy) % NY) * NZ + zh))
    greet(at_out(y * NZ + 1 - zh))
    pl.when(has_up)(lambda: greet(at_inp(zi + 1)))
    pl.when(has_dn)(lambda: greet(at_inp(zi - 1)))
    ends = jnp.where(has_up, 1, 0) + jnp.where(has_dn, 1, 0)
    pl.semaphore_wait(barrier, 1 + (NX - 1) + (NY - 1) + 1 + ends)

    def gather_tok(buf, ss, rs, pieces):
        step = ts // pieces

        def copy(k, slot, dev, c):
            part = buf.at[pl.ds(pl.multiple_of(k * ts + c * step, step), step)]
            return rc(part, part, ss.at[slot, c], rs.at[k, c], dev)

        near = [1, -1][: min(NX - 1, 2)]

        def sends():
            yield 0, (t, 0, at_tok(sib))
            for i, dx in enumerate(near):
                yield 0, (t, 1 + i, at_tok(tok_of(dx)))
            for i, dx in enumerate(near):
                yield 1, (tok_of(dx), 3 + i, at_tok(sib))
            if NX > 2:
                yield 1, (tok_of(2 * core - 1), 5, at_tok(tok_of(1 - 2 * core)))
                yield 2, (tok_of(2), 6, at_tok(sib))

        def arrived(k, c):
            copy(k, 0, at_tok(sib), c).wait_recv()

        def start(stage, c):
            for at, args in sends():
                if at == stage:
                    copy(*args, c).start()

        def begin():
            for c in range(pieces):
                start(0, c)

        def middle():
            for c in range(pieces):
                for dx in near:
                    arrived(tok_of(dx), c)
                start(1, c)

        def end():
            for c in range(pieces):
                if NX > 2:
                    arrived(tok_of(2), c)
                    start(2, c)
            for c in range(pieces):
                for dx in range(NX):
                    arrived(((x + dx) % NX) * NC + 1 - core, c)

        def drain():
            for c in range(pieces):
                for _, args in sends():
                    copy(*args, c).wait_send()

        return begin, middle, end, drain

    def hand(buf, ss, rs, j, c, up):
        return rc(buf.at[j, c], buf.at[j, c], ss.at[up, j, c], rs.at[j, c], at_inp(zi + 1 if up else zi - 1))

    def own_both(buf, ss, rs, c):
        pl.when(has_up)(lambda: hand(buf, ss, rs, zi, c, 1).start())
        pl.when(has_dn)(lambda: hand(buf, ss, rs, zi, c, 0).start())

    def pass_on(buf, ss, rs, s, c):
        @pl.when(zi + s <= NI - 1)
        def _():
            hand(buf, ss, rs, zi + s, c, 1).wait_recv()
            pl.when(has_dn)(lambda: hand(buf, ss, rs, zi + s, c, 0).start())

        @pl.when(zi - s >= 0)
        def _():
            hand(buf, ss, rs, zi - s, c, 0).wait_recv()
            pl.when(has_up)(lambda: hand(buf, ss, rs, zi - s, c, 1).start())

    def drain_z(buf, ss, rs, pieces):
        def body(j, carry):
            for c in range(pieces):
                pl.when(jnp.logical_and(has_up, j <= zi))(lambda c=c: hand(buf, ss, rs, j, c, 1).wait_send())
                pl.when(jnp.logical_and(has_dn, j >= zi))(lambda c=c: hand(buf, ss, rs, j, c, 0).wait_send())
            return carry

        lax.fori_loop(0, NI, body, 0)

    def order(n):
        m = jnp.minimum(zi, NI - 1 - zi)
        half = (n + 1) // 2
        near = jnp.where(n % 2 == 1, zi + half, zi - half)
        far = jnp.where(zi <= m, n, NI - 1 - n)
        return jnp.where(n <= 2 * m, near, far)

    def block(buf, j):
        return buf[pl.ds(pl.multiple_of(j * tb, tb), tb), :]

    def chain(buf, ss, rs, d, c, up):
        return rc(buf.at[d, c], buf.at[d, c], ss.at[d, c], rs.at[d, c], at_inp(zi + 1 if up else zi - 1))

    def up_on(k):
        return jnp.logical_and(zi <= k, has_up)

    def dn_on(k):
        return jnp.logical_and(k >= NI - 1 - zi, has_dn)

    def up_dst(k):
        return NI - 1 - k + zi

    def dn_dst(k):
        return k - (NI - 1 - zi)

    def products(k):
        @pl.when(up_on(k))
        def _():
            PU[...] = dot(WD[...], block(GA, up_dst(k)), LAST)

        @pl.when(dn_on(k))
        def _():
            PD[...] = dot(WD[...], block(GA, dn_dst(k)), LAST)

    def slot(k):
        for c in range(CH):
            piece = slice(c * fc, (c + 1) * fc)

            @pl.when(up_on(k))
            def _():
                d = up_dst(k)

                @pl.when(has_dn)
                def _():
                    chain(RU, ru_s, ru_r, d, c, 1).wait_recv()
                    RU[d, c] = (PU[piece, :] + RU[d, c].astype(F32)).astype(BF16)

                @pl.when(jnp.logical_not(has_dn))
                def _():
                    RU[d, c] = PU[piece, :].astype(BF16)

                chain(RU, ru_s, ru_r, d, c, 1).start()

            @pl.when(dn_on(k))
            def _():
                d = dn_dst(k)

                @pl.when(has_up)
                def _():
                    chain(RD, rd_s, rd_r, d, c, 0).wait_recv()
                    RD[d, c] = (PD[piece, :] + RD[d, c].astype(F32)).astype(BF16)

                @pl.when(jnp.logical_not(has_up))
                def _():
                    RD[d, c] = PD[piece, :].astype(BF16)

                chain(RD, rd_s, rd_r, d, c, 0).start()

    def last_hop(c, up):
        return rc(FS.at[up, c], FR.at[up, c], fr_s.at[up, c], fr_r.at[up, c], at_inp(zi + 1 if up else zi - 1))

    def last_slot():
        for c in range(CH):
            piece = slice(c * fc, (c + 1) * fc)

            @pl.when(has_up)
            def _():
                @pl.when(has_dn)
                def _():
                    chain(RU, ru_s, ru_r, zi + 1, c, 1).wait_recv()
                    PU[piece, :] += RU[zi + 1, c].astype(F32)

                FS[1, c] = PU[piece, :].astype(FS.dtype)
                last_hop(c, 1).start()

            @pl.when(has_dn)
            def _():
                @pl.when(has_up)
                def _():
                    chain(RD, rd_s, rd_r, zi - 1, c, 0).wait_recv()
                    PD[piece, :] += RD[zi - 1, c].astype(F32)

                FS[0, c] = PD[piece, :].astype(FS.dtype)
                last_hop(c, 0).start()

    def close_chains(c):
        piece = slice(c * fc, (c + 1) * fc)

        @pl.when(has_dn)
        def _():
            last_hop(c, 1).wait_recv()
            PO[piece, :] += FR[1, c].astype(F32)

        @pl.when(has_up)
        def _():
            last_hop(c, 0).wait_recv()
            PO[piece, :] += FR[0, c].astype(F32)

        H[zi, c] = PO[piece, :].astype(BF16)

    def drain_chains():
        def body(d, carry):
            for c in range(CH):
                pl.when(d > zi + 1)(lambda c=c: chain(RU, ru_s, ru_r, d, c, 1).wait_send())
                pl.when(d < zi - 1)(lambda c=c: chain(RD, rd_s, rd_r, d, c, 0).wait_send())
            return carry

        lax.fori_loop(0, NI, body, 0)
        for c in range(CH):
            pl.when(has_up)(lambda c=c: last_hop(c, 1).wait_send())
            pl.when(has_dn)(lambda c=c: last_hop(c, 0).wait_send())

    def terms(n):
        j = order(n)
        g, u = GU[j, 0].astype(F32), GU[j, 1].astype(F32)
        sig = 1.0 / (1.0 + jnp.exp(-g))
        gs = g * sig
        TA[n] = u * sig * (1.0 + g * (1.0 - sig))
        TB[n] = gs
        HD[n] = (gs * u).astype(BF16)

    def grads(n):
        j = order(n)
        h = H[j].reshape(F, tb).astype(F32)
        gg, ug = (h * TA[n]).astype(BF16), (h * TB[n]).astype(BF16)
        part = dot(gg, WG[...], LEAD) + dot(ug, WU[...], LEAD)
        part = part.reshape(NX, NC, rows, D)
        for c in range(NC):
            IG2[c, n] = part[:, c]
        ig_core(n).start()
        xb = block(XA, j)
        GW[...] += dot(gg, xb)
        UW[...] += dot(ug, xb)
        DW[...] += dot(HD[n], block(GA, j))

    def ig_core(n):
        return rc(IG2.at[1 - core, n], IGR.at[n], ig_s.at[n], ig_r.at[n], at_tok(sib))

    def ig_x(n, dx):
        return rc(
            XB.at[n, (x + dx) % NX], XR.at[dx - 1, n], xs_s.at[dx - 1, n], xs_r.at[dx - 1, n], at_tok(tok_of(dx))
        )

    def ig_y(n):
        j = order(n)
        root = j // NZ
        far = (y - root + NY) % NY - 1
        return rc(YS.at[j], YR.at[far, j % NZ], ys_s.at[n], ys_r.at[far, j % NZ], at_out(root * NZ + zh))

    def ig_z():
        j = y * NZ + 1 - zh
        return rc(ZS, ZR, z_s, z_r, at_out(j))

    def sum_core(n):
        ig_core(n).wait()
        XS[n] = IG2[core, n] + IGR[n]
        XB[n] = XS[n].astype(BF16)
        for dx in range(1, NX):
            ig_x(n, dx).start()

    def sum_x(n):
        total = XS[n, x]
        for dx in range(1, NX):
            ig_x(n, dx).wait()
            total = total + XR[dx - 1, n].astype(F32)
        YS[order(n)] = total
        pl.when(y != order(n) // NZ)(lambda: ig_y(n).start())

    def sum_y(n):
        j = order(n)

        @pl.when(y != j // NZ)
        def _():
            ig_y(n).wait_send()

        @pl.when(y == j // NZ)
        def _():
            total = YS[j]
            for far in range(NY - 1):
                rc(YS.at[j], YR.at[far, j % NZ], ys_s.at[n], ys_r.at[far, j % NZ], at_out(y * NZ + 1 - zh)).wait_recv()
                total = total + YR[far, j % NZ]
            YS[j] = total

            @pl.when(zh != j % NZ)
            def _():
                ZS[...] = total.astype(ZS.dtype)
                ig_z().start()

    loads[0].wait()
    g_begin, g_middle, g_end, g_drain = gather_tok(GA, ga_s, ga_r, TP)
    g_begin()
    loads[1].wait()
    GU[zi, 0] = GF[...].astype(BF16)
    own_both(GU, gu_s, gu_r, 0)
    loads[2].wait()
    GU[zi, 1] = UF[...].astype(BF16)
    own_both(GU, gu_s, gu_r, 1)
    loads[3].wait()
    XA[pl.ds(pl.multiple_of(t * ts, ts), ts), :] = XF[...].astype(BF16)
    x_begin, x_middle, x_end, x_drain = gather_tok(XA, xa_s, xa_r, TP)

    def gu_event(e):
        pl.when(e < 2 * (NI - 1))(lambda: pass_on(GU, gu_s, gu_r, e // 2 + 1, e % 2))

    GW[...] = jnp.zeros_like(GW)
    UW[...] = jnp.zeros_like(UW)
    DW[...] = jnp.zeros_like(DW)
    for c in loads[4:]:
        c.wait()
    g_middle()
    x_begin()
    for e in range(E0):
        gu_event(e)
    g_end()
    products(0)

    def rs_step(k, carry):
        slot(k)
        gu_event(E0 + k)
        products(k + 1)
        pl.when(k == XM)(x_middle)
        pl.when(k == XE)(x_end)
        pl.when(k >= 2)(lambda: terms(k - 2))
        return carry

    lax.fori_loop(0, NI - 2, rs_step, 0)
    last_slot()
    gu_event(E0 + NI - 2)
    if XM > NI - 3:
        x_middle()
    if XE > NI - 3:
        x_end()
    first_terms = max(NI - 4, 0)
    PO[...] = dot(WD[...], block(GA, zi), LAST)
    for c in range(CH):
        close_chains(c)
        own_both(H, h_s, h_r, c)
    events = E0 + NI - 1

    def h_step(s, carry):
        for c in range(CH):
            pass_on(H, h_s, h_r, s, c)
            if c == 0:
                gu_event(events + s - 1)
        for n in range(first_terms, NI):
            pl.when(s == max(n - first_terms, 2 * n - events, 1))(lambda n=n: terms(n))
        pl.when(s == 1)(lambda: grads(0))
        sum_core(s - 1)
        pl.when(s >= 2)(lambda: sum_x(s - 2))
        pl.when(s >= 3)(lambda: sum_y(s - 3))
        grads(s)
        return carry

    lax.fori_loop(1, NI, h_step, 0)
    sum_core(NI - 1)
    sum_x(NI - 2)
    gw_out[...] = GW[...].astype(BF16)
    if NI > 2:
        sum_y(NI - 3)
    sum_x(NI - 1)
    sum_y(NI - 2)
    uw_out[...] = UW[...].astype(BF16)
    sum_y(NI - 1)
    dw_out[...] = DW[...].astype(BF16)
    g_drain()
    x_drain()
    drain_z(GU, gu_s, gu_r, 2)
    drain_z(H, h_s, h_r, CH)
    drain_chains()
    ig_z().wait()
    ig_ref[...] = (YS[o] + ZR[...].astype(F32)).astype(BF16)


def copy_out(*refs):
    n = len(refs) // 2
    copies = [pltpu.make_async_copy(refs[i], refs[n + i], refs[-1].at[i]) for i in range(n)]
    for c in copies:
        c.start()
    for c in copies:
        c.wait()


def local(saved_input, saved_gate, saved_up, out_grad, w_gate, w_up, w_down):
    sizes = tuple(lax.axis_size(a) for a in ("inp", "out", "tok"))
    NI, NO, NT = sizes
    NX, NY = NT // NC, NO // NZ
    ts, D = saved_input.shape
    tb, F = saved_gate.shape
    T = tb * NI
    rows = tb // NT
    dma = pltpu.SemaphoreType.DMA
    vmem = pl.BlockSpec(memory_space=pltpu.VMEM)
    anyw = pl.BlockSpec(memory_space=pl.ANY)
    fc = F // CH
    ig, gw, uw, dw = pl.pallas_call(
        functools.partial(kernel, sizes),
        out_shape=(
            pltpu.VMEM((rows, D), BF16),
            pltpu.VMEM((F, D), BF16),
            pltpu.VMEM((F, D), BF16),
            pltpu.VMEM((F, D), BF16),
        ),
        in_specs=[anyw] * 7,
        out_specs=(vmem,) * 4,
        scratch_shapes=[
            pltpu.VMEM((ts, D), F32),
            pltpu.VMEM((F, tb), F32),
            pltpu.VMEM((F, tb), F32),
            pltpu.VMEM((F, D), BF16),
            pltpu.VMEM((F, D), BF16),
            pltpu.VMEM((F, D), BF16),
            pltpu.VMEM((T, D), BF16),
            pltpu.VMEM((T, D), BF16),
            pltpu.VMEM((NI, 2, F, tb), BF16),
            pltpu.VMEM((NI, CH, fc, tb), BF16),
            pltpu.VMEM((NI, CH, fc, tb), BF16),
            pltpu.VMEM((NI, CH, fc, tb), BF16),
            pltpu.VMEM((F, tb), F32),
            pltpu.VMEM((F, tb), F32),
            pltpu.VMEM((F, tb), F32),
            pltpu.VMEM((NI, F, tb), F32),
            pltpu.VMEM((NI, F, tb), F32),
            pltpu.VMEM((NI, F, tb), BF16),
            pltpu.VMEM((F, D), F32),
            pltpu.VMEM((F, D), F32),
            pltpu.VMEM((F, D), F32),
            pltpu.VMEM((2, CH, fc, tb), LAST_HOP),
            pltpu.VMEM((2, CH, fc, tb), LAST_HOP),
            pltpu.VMEM((NC, NI, NX, rows, D), F32),
            pltpu.VMEM((NI, NX, rows, D), F32),
            pltpu.VMEM((NI, NX, rows, D), F32),
            pltpu.VMEM((NI, NX, rows, D), BF16),
            pltpu.VMEM((max(NX - 1, 1), NI, rows, D), BF16),
            pltpu.VMEM((NO, rows, D), F32),
            pltpu.VMEM((max(NY - 1, 1), NZ, rows, D), F32),
            pltpu.VMEM((rows, D), Z_HOP),
            pltpu.VMEM((rows, D), Z_HOP),
            dma((7,)),
            dma((7, TP)), dma((NT, TP)), dma((7, TP)), dma((NT, TP)),
            dma((2, NI, 2)), dma((NI, 2)), dma((2, NI, CH)), dma((NI, CH)),
            dma((NI, CH)), dma((NI, CH)), dma((NI, CH)), dma((NI, CH)), dma((2, CH)), dma((2, CH)),
            dma((NI,)), dma((NI,)),
            dma((max(NX - 1, 1), NI)), dma((max(NX - 1, 1), NI)),
            dma((NI,)), dma((max(NY - 1, 1), NZ)), dma, dma,
        ],
        compiler_params=pltpu.CompilerParams(
            collective_id=0, has_side_effects=True, vmem_limit_bytes=56 * 1024 * 1024
        ),
    )(saved_input, saved_gate.T, saved_up.T, out_grad, w_gate.T, w_up.T, w_down)
    results = (ig, gw, uw, dw)
    ig, gw, uw, dw = pl.pallas_call(
        copy_out,
        out_shape=tuple(jax.ShapeDtypeStruct(r.shape, r.dtype) for r in results),
        in_specs=[vmem] * 4,
        out_specs=(anyw,) * 4,
        scratch_shapes=[dma((4,))],
    )(*[pltpu.with_memory_space_constraint(r, pltpu.VMEM) for r in results])
    return ig, gw.T, uw.T, dw


def solution(mesh):
    placed = (
        P("tok", "inp"),
        P("inp", ("out", "tok")),
        P("inp", ("out", "tok")),
        P("tok", "inp"),
        P("inp", ("out", "tok")),
        P("inp", ("out", "tok")),
        P(("out", "tok"), "inp"),
    )
    return jax.shard_map(
        local,
        mesh=mesh,
        in_specs=placed,
        out_specs=(
            P(("out", "tok"), "inp"),
            P("inp", ("out", "tok")),
            P("inp", ("out", "tok")),
            P(("out", "tok"), "inp"),
        ),
        check_vma=False,
    )
```

```python
import functools

import jax
import jax.numpy as jnp
from jax import lax
from jax.experimental import pallas as pl
from jax.experimental.pallas import tpu as pltpu
from jax.sharding import PartitionSpec as P

MESH = pl.DeviceIdType.MESH
F32 = jnp.float32
BF16 = jnp.bfloat16
LAST = (((1,), (1,)), ((), ()))
LEAD = (((0,), (0,)), ((), ()))
NC = 2
NZ = 2
CH = 4
TP = 1
XM, XE = 3, 5
LAST_HOP = BF16
Z_HOP = F32
E0 = 4


def dot(a, b, dims=(((1,), (0,)), ((), ()))):
    return lax.dot_general(a, b, dims, preferred_element_type=F32)


def kernel(
    sizes,
    x_in, g_in, u_in, go_in, wg_in, wu_in, wd_in,
    ig_ref, gw_out, uw_out, dw_out,
    XF, GF, UF, WG, WU, WD,
    GA, XA, GU, H, RU, RD, PU, PD, PO, TA, TB, HD, GW, UW, DW, FS, FR,
    IG2, IGR, XS, XB, XR, YS, YR, ZS, ZR,
    in_s, ga_s, ga_r, xa_s, xa_r, gu_s, gu_r, h_s, h_r, ru_s, ru_r, rd_s, rd_r, fr_s, fr_r,
    ig_s, ig_r, xs_s, xs_r, ys_s, ys_r, z_s, z_r,
):
    NI, NO, NT = sizes
    NX, NY = NT // NC, NO // NZ
    zi, o, t = lax.axis_index("inp"), lax.axis_index("out"), lax.axis_index("tok")
    x, core = t // NC, t % NC
    y, zh = o // NZ, o % NZ
    F, tb = g_in.shape
    ts, D = go_in.shape
    fc = F // CH
    rows = tb // NT

    def at_inp(k):
        return {"inp": k}

    def at_tok(k):
        return {"tok": k}

    def at_out(k):
        return {"out": k}

    def rc(src, dst, ss, rs, dev):
        return pltpu.make_async_remote_copy(
            src_ref=src, dst_ref=dst, send_sem=ss, recv_sem=rs, device_id=dev, device_id_type=MESH
        )

    has_up, has_dn = zi < NI - 1, zi > 0
    sib = x * NC + (1 - core)

    def tok_of(dx):
        return ((x + dx + NX) % NX) * NC + core

    def rows_of(buf, k):
        return buf.at[pl.ds(pl.multiple_of(k * ts, ts), ts)]

    loads = [
        pltpu.make_async_copy(src, dst, in_s.at[i])
        for i, (src, dst) in enumerate(
            [(go_in, rows_of(GA, t)), (g_in, GF), (u_in, UF), (x_in, XF), (wd_in, WD), (wg_in, WG), (wu_in, WU)]
        )
    ]
    for c in loads:
        c.start()

    barrier = pltpu.get_barrier_semaphore()

    def greet(dev):
        pl.semaphore_signal(barrier, inc=1, device_id=dev, device_id_type=MESH)

    greet(at_tok(sib))
    for dx in range(1, NX):
        greet(at_tok(tok_of(dx)))
    for dy in range(1, NY):
        greet(at_out(((y + dy) % NY) * NZ + zh))
    greet(at_out(y * NZ + 1 - zh))
    pl.when(has_up)(lambda: greet(at_inp(zi + 1)))
    pl.when(has_dn)(lambda: greet(at_inp(zi - 1)))
    ends = jnp.where(has_up, 1, 0) + jnp.where(has_dn, 1, 0)
    loads[1].wait()
    GU[zi, 0] = GF[...].astype(BF16)
    loads[2].wait()
    GU[zi, 1] = UF[...].astype(BF16)
    loads[3].wait()
    XA[pl.ds(pl.multiple_of(t * ts, ts), ts), :] = XF[...].astype(BF16)
    loads[0].wait()
    pl.semaphore_wait(barrier, 1 + (NX - 1) + (NY - 1) + 1 + ends)

    def gather_tok(buf, ss, rs, pieces):
        step = ts // pieces

        def copy(k, slot, dev, c):
            part = buf.at[pl.ds(pl.multiple_of(k * ts + c * step, step), step)]
            return rc(part, part, ss.at[slot, c], rs.at[k, c], dev)

        near = [1, -1][: min(NX - 1, 2)]

        def sends():
            yield 0, (t, 0, at_tok(sib))
            for i, dx in enumerate(near):
                yield 0, (t, 1 + i, at_tok(tok_of(dx)))
            for i, dx in enumerate(near):
                yield 1, (tok_of(dx), 3 + i, at_tok(sib))
            if NX > 2:
                yield 1, (tok_of(2 * core - 1), 5, at_tok(tok_of(1 - 2 * core)))
                yield 2, (tok_of(2), 6, at_tok(sib))

        def arrived(k, c):
            copy(k, 0, at_tok(sib), c).wait_recv()

        def start(stage, c):
            for at, args in sends():
                if at == stage:
                    copy(*args, c).start()

        def begin():
            for c in range(pieces):
                start(0, c)

        def middle():
            for c in range(pieces):
                for dx in near:
                    arrived(tok_of(dx), c)
                start(1, c)

        def end():
            for c in range(pieces):
                if NX > 2:
                    arrived(tok_of(2), c)
                    start(2, c)
            for c in range(pieces):
                for dx in range(NX):
                    arrived(((x + dx) % NX) * NC + 1 - core, c)

        def drain():
            for c in range(pieces):
                for _, args in sends():
                    copy(*args, c).wait_send()

        return begin, middle, end, drain

    def hand(buf, ss, rs, j, c, up):
        return rc(buf.at[j, c], buf.at[j, c], ss.at[up, j, c], rs.at[j, c], at_inp(zi + 1 if up else zi - 1))

    def own_both(buf, ss, rs, c):
        pl.when(has_up)(lambda: hand(buf, ss, rs, zi, c, 1).start())
        pl.when(has_dn)(lambda: hand(buf, ss, rs, zi, c, 0).start())

    def pass_on(buf, ss, rs, s, c):
        @pl.when(zi + s <= NI - 1)
        def _():
            hand(buf, ss, rs, zi + s, c, 1).wait_recv()
            pl.when(has_dn)(lambda: hand(buf, ss, rs, zi + s, c, 0).start())

        @pl.when(zi - s >= 0)
        def _():
            hand(buf, ss, rs, zi - s, c, 0).wait_recv()
            pl.when(has_up)(lambda: hand(buf, ss, rs, zi - s, c, 1).start())

    def drain_z(buf, ss, rs, pieces):
        def body(j, carry):
            for c in range(pieces):
                pl.when(jnp.logical_and(has_up, j <= zi))(lambda c=c: hand(buf, ss, rs, j, c, 1).wait_send())
                pl.when(jnp.logical_and(has_dn, j >= zi))(lambda c=c: hand(buf, ss, rs, j, c, 0).wait_send())
            return carry

        lax.fori_loop(0, NI, body, 0)

    def order(n):
        m = jnp.minimum(zi, NI - 1 - zi)
        half = (n + 1) // 2
        near = jnp.where(n % 2 == 1, zi + half, zi - half)
        far = jnp.where(zi <= m, n, NI - 1 - n)
        return jnp.where(n <= 2 * m, near, far)

    def block(buf, j):
        return buf[pl.ds(pl.multiple_of(j * tb, tb), tb), :]

    def chain(buf, ss, rs, d, c, up):
        return rc(buf.at[d, c], buf.at[d, c], ss.at[d, c], rs.at[d, c], at_inp(zi + 1 if up else zi - 1))

    def up_on(k):
        return jnp.logical_and(zi <= k, has_up)

    def dn_on(k):
        return jnp.logical_and(k >= NI - 1 - zi, has_dn)

    def up_dst(k):
        return NI - 1 - k + zi

    def dn_dst(k):
        return k - (NI - 1 - zi)

    def products(k):
        @pl.when(up_on(k))
        def _():
            PU[...] = dot(WD[...], block(GA, up_dst(k)), LAST)

        @pl.when(dn_on(k))
        def _():
            PD[...] = dot(WD[...], block(GA, dn_dst(k)), LAST)

    def slot(k):
        for c in range(CH):
            piece = slice(c * fc, (c + 1) * fc)

            @pl.when(up_on(k))
            def _():
                d = up_dst(k)

                @pl.when(has_dn)
                def _():
                    chain(RU, ru_s, ru_r, d, c, 1).wait_recv()
                    RU[d, c] = (PU[piece, :] + RU[d, c].astype(F32)).astype(BF16)

                @pl.when(jnp.logical_not(has_dn))
                def _():
                    RU[d, c] = PU[piece, :].astype(BF16)

                chain(RU, ru_s, ru_r, d, c, 1).start()

            @pl.when(dn_on(k))
            def _():
                d = dn_dst(k)

                @pl.when(has_up)
                def _():
                    chain(RD, rd_s, rd_r, d, c, 0).wait_recv()
                    RD[d, c] = (PD[piece, :] + RD[d, c].astype(F32)).astype(BF16)

                @pl.when(jnp.logical_not(has_up))
                def _():
                    RD[d, c] = PD[piece, :].astype(BF16)

                chain(RD, rd_s, rd_r, d, c, 0).start()

    def last_hop(c, up):
        return rc(FS.at[up, c], FR.at[up, c], fr_s.at[up, c], fr_r.at[up, c], at_inp(zi + 1 if up else zi - 1))

    def last_slot():
        for c in range(CH):
            piece = slice(c * fc, (c + 1) * fc)

            @pl.when(has_up)
            def _():
                @pl.when(has_dn)
                def _():
                    chain(RU, ru_s, ru_r, zi + 1, c, 1).wait_recv()
                    PU[piece, :] += RU[zi + 1, c].astype(F32)

                FS[1, c] = PU[piece, :].astype(FS.dtype)
                last_hop(c, 1).start()

            @pl.when(has_dn)
            def _():
                @pl.when(has_up)
                def _():
                    chain(RD, rd_s, rd_r, zi - 1, c, 0).wait_recv()
                    PD[piece, :] += RD[zi - 1, c].astype(F32)

                FS[0, c] = PD[piece, :].astype(FS.dtype)
                last_hop(c, 0).start()

    def close_chains(c):
        piece = slice(c * fc, (c + 1) * fc)

        @pl.when(has_dn)
        def _():
            last_hop(c, 1).wait_recv()
            PO[piece, :] += FR[1, c].astype(F32)

        @pl.when(has_up)
        def _():
            last_hop(c, 0).wait_recv()
            PO[piece, :] += FR[0, c].astype(F32)

        H[zi, c] = PO[piece, :].astype(BF16)

    def drain_chains():
        def body(d, carry):
            for c in range(CH):
                pl.when(d > zi + 1)(lambda c=c: chain(RU, ru_s, ru_r, d, c, 1).wait_send())
                pl.when(d < zi - 1)(lambda c=c: chain(RD, rd_s, rd_r, d, c, 0).wait_send())
            return carry

        lax.fori_loop(0, NI, body, 0)
        for c in range(CH):
            pl.when(has_up)(lambda c=c: last_hop(c, 1).wait_send())
            pl.when(has_dn)(lambda c=c: last_hop(c, 0).wait_send())

    def terms(n):
        j = order(n)
        g, u = GU[j, 0].astype(F32), GU[j, 1].astype(F32)
        sig = 1.0 / (1.0 + jnp.exp(-g))
        gs = g * sig
        TA[n] = u * sig * (1.0 + g * (1.0 - sig))
        TB[n] = gs
        HD[n] = (gs * u).astype(BF16)

    def grads(n):
        j = order(n)
        h = H[j].reshape(F, tb).astype(F32)
        gg, ug = (h * TA[n]).astype(BF16), (h * TB[n]).astype(BF16)
        part = dot(gg, WG[...], LEAD) + dot(ug, WU[...], LEAD)
        part = part.reshape(NX, NC, rows, D)
        for c in range(NC):
            IG2[c, n] = part[:, c]
        ig_core(n).start()
        xb = block(XA, j)
        GW[...] += dot(gg, xb)
        UW[...] += dot(ug, xb)
        DW[...] += dot(HD[n], block(GA, j))

    def ig_core(n):
        return rc(IG2.at[1 - core, n], IGR.at[n], ig_s.at[n], ig_r.at[n], at_tok(sib))

    def ig_x(n, dx):
        return rc(
            XB.at[n, (x + dx) % NX], XR.at[dx - 1, n], xs_s.at[dx - 1, n], xs_r.at[dx - 1, n], at_tok(tok_of(dx))
        )

    def ig_y(n):
        j = order(n)
        root = j // NZ
        far = (y - root + NY) % NY - 1
        return rc(YS.at[j], YR.at[far, j % NZ], ys_s.at[n], ys_r.at[far, j % NZ], at_out(root * NZ + zh))

    def ig_z():
        j = y * NZ + 1 - zh
        return rc(ZS, ZR, z_s, z_r, at_out(j))

    def sum_core(n):
        ig_core(n).wait()
        XS[n] = IG2[core, n] + IGR[n]
        XB[n] = XS[n].astype(BF16)
        for dx in range(1, NX):
            ig_x(n, dx).start()

    def sum_x(n):
        total = XS[n, x]
        for dx in range(1, NX):
            ig_x(n, dx).wait()
            total = total + XR[dx - 1, n].astype(F32)
        YS[order(n)] = total
        pl.when(y != order(n) // NZ)(lambda: ig_y(n).start())

    def sum_y(n):
        j = order(n)

        @pl.when(y != j // NZ)
        def _():
            ig_y(n).wait_send()

        @pl.when(y == j // NZ)
        def _():
            total = YS[j]
            for far in range(NY - 1):
                rc(YS.at[j], YR.at[far, j % NZ], ys_s.at[n], ys_r.at[far, j % NZ], at_out(y * NZ + 1 - zh)).wait_recv()
                total = total + YR[far, j % NZ]
            YS[j] = total

            @pl.when(zh != j % NZ)
            def _():
                ZS[...] = total.astype(ZS.dtype)
                ig_z().start()

    g_begin, g_middle, g_end, g_drain = gather_tok(GA, ga_s, ga_r, TP)
    g_begin()
    own_both(GU, gu_s, gu_r, 0)
    own_both(GU, gu_s, gu_r, 1)
    x_begin, x_middle, x_end, x_drain = gather_tok(XA, xa_s, xa_r, TP)

    def gu_event(e):
        pl.when(e < 2 * (NI - 1))(lambda: pass_on(GU, gu_s, gu_r, e // 2 + 1, e % 2))

    GW[...] = jnp.zeros_like(GW)
    UW[...] = jnp.zeros_like(UW)
    DW[...] = jnp.zeros_like(DW)
    for c in loads[4:]:
        c.wait()
    g_middle()
    x_begin()
    for e in range(E0):
        gu_event(e)
    g_end()
    products(0)

    def rs_step(k, carry):
        slot(k)
        gu_event(E0 + k)
        products(k + 1)
        pl.when(k == XM)(x_middle)
        pl.when(k == XE)(x_end)
        pl.when(k >= 2)(lambda: terms(k - 2))
        return carry

    lax.fori_loop(0, NI - 2, rs_step, 0)
    last_slot()
    gu_event(E0 + NI - 2)
    if XM > NI - 3:
        x_middle()
    if XE > NI - 3:
        x_end()
    first_terms = max(NI - 4, 0)
    PO[...] = dot(WD[...], block(GA, zi), LAST)
    for c in range(CH):
        close_chains(c)
        own_both(H, h_s, h_r, c)
    events = E0 + NI - 1

    def h_step(s, carry):
        for c in range(CH):
            pass_on(H, h_s, h_r, s, c)
            if c == 0:
                gu_event(events + s - 1)
        for n in range(first_terms, NI):
            pl.when(s == max(n - first_terms, 2 * n - events, 1))(lambda n=n: terms(n))
        pl.when(s == 1)(lambda: grads(0))
        sum_core(s - 1)
        pl.when(s >= 2)(lambda: sum_x(s - 2))
        pl.when(s >= 3)(lambda: sum_y(s - 3))
        grads(s)
        return carry

    lax.fori_loop(1, NI, h_step, 0)
    sum_core(NI - 1)
    sum_x(NI - 2)
    gw_out[...] = GW[...].astype(BF16)
    if NI > 2:
        sum_y(NI - 3)
    sum_x(NI - 1)
    sum_y(NI - 2)
    uw_out[...] = UW[...].astype(BF16)
    sum_y(NI - 1)
    dw_out[...] = DW[...].astype(BF16)
    g_drain()
    x_drain()
    drain_z(GU, gu_s, gu_r, 2)
    drain_z(H, h_s, h_r, CH)
    drain_chains()
    ig_z().wait()
    ig_ref[...] = (YS[o] + ZR[...].astype(F32)).astype(BF16)


def copy_out(*refs):
    n = len(refs) // 2
    copies = [pltpu.make_async_copy(refs[i], refs[n + i], refs[-1].at[i]) for i in range(n)]
    for c in copies:
        c.start()
    for c in copies:
        c.wait()


def local(saved_input, saved_gate, saved_up, out_grad, w_gate, w_up, w_down):
    sizes = tuple(lax.axis_size(a) for a in ("inp", "out", "tok"))
    NI, NO, NT = sizes
    NX, NY = NT // NC, NO // NZ
    ts, D = saved_input.shape
    tb, F = saved_gate.shape
    T = tb * NI
    rows = tb // NT
    dma = pltpu.SemaphoreType.DMA
    vmem = pl.BlockSpec(memory_space=pltpu.VMEM)
    anyw = pl.BlockSpec(memory_space=pl.ANY)
    fc = F // CH
    ig, gw, uw, dw = pl.pallas_call(
        functools.partial(kernel, sizes),
        out_shape=(
            pltpu.VMEM((rows, D), BF16),
            pltpu.VMEM((F, D), BF16),
            pltpu.VMEM((F, D), BF16),
            pltpu.VMEM((F, D), BF16),
        ),
        in_specs=[anyw] * 7,
        out_specs=(vmem,) * 4,
        scratch_shapes=[
            pltpu.VMEM((ts, D), F32),
            pltpu.VMEM((F, tb), F32),
            pltpu.VMEM((F, tb), F32),
            pltpu.VMEM((F, D), BF16),
            pltpu.VMEM((F, D), BF16),
            pltpu.VMEM((F, D), BF16),
            pltpu.VMEM((T, D), BF16),
            pltpu.VMEM((T, D), BF16),
            pltpu.VMEM((NI, 2, F, tb), BF16),
            pltpu.VMEM((NI, CH, fc, tb), BF16),
            pltpu.VMEM((NI, CH, fc, tb), BF16),
            pltpu.VMEM((NI, CH, fc, tb), BF16),
            pltpu.VMEM((F, tb), F32),
            pltpu.VMEM((F, tb), F32),
            pltpu.VMEM((F, tb), F32),
            pltpu.VMEM((NI, F, tb), F32),
            pltpu.VMEM((NI, F, tb), F32),
            pltpu.VMEM((NI, F, tb), BF16),
            pltpu.VMEM((F, D), F32),
            pltpu.VMEM((F, D), F32),
            pltpu.VMEM((F, D), F32),
            pltpu.VMEM((2, CH, fc, tb), LAST_HOP),
            pltpu.VMEM((2, CH, fc, tb), LAST_HOP),
            pltpu.VMEM((NC, NI, NX, rows, D), F32),
            pltpu.VMEM((NI, NX, rows, D), F32),
            pltpu.VMEM((NI, NX, rows, D), F32),
            pltpu.VMEM((NI, NX, rows, D), BF16),
            pltpu.VMEM((max(NX - 1, 1), NI, rows, D), BF16),
            pltpu.VMEM((NO, rows, D), F32),
            pltpu.VMEM((max(NY - 1, 1), NZ, rows, D), F32),
            pltpu.VMEM((rows, D), Z_HOP),
            pltpu.VMEM((rows, D), Z_HOP),
            dma((7,)),
            dma((7, TP)), dma((NT, TP)), dma((7, TP)), dma((NT, TP)),
            dma((2, NI, 2)), dma((NI, 2)), dma((2, NI, CH)), dma((NI, CH)),
            dma((NI, CH)), dma((NI, CH)), dma((NI, CH)), dma((NI, CH)), dma((2, CH)), dma((2, CH)),
            dma((NI,)), dma((NI,)),
            dma((max(NX - 1, 1), NI)), dma((max(NX - 1, 1), NI)),
            dma((NI,)), dma((max(NY - 1, 1), NZ)), dma, dma,
        ],
        compiler_params=pltpu.CompilerParams(
            collective_id=0, has_side_effects=True, vmem_limit_bytes=56 * 1024 * 1024
        ),
    )(saved_input, saved_gate.T, saved_up.T, out_grad, w_gate.T, w_up.T, w_down)
    results = (ig, gw, uw, dw)
    ig, gw, uw, dw = pl.pallas_call(
        copy_out,
        out_shape=tuple(jax.ShapeDtypeStruct(r.shape, r.dtype) for r in results),
        in_specs=[vmem] * 4,
        out_specs=(anyw,) * 4,
        scratch_shapes=[dma((4,))],
    )(*[pltpu.with_memory_space_constraint(r, pltpu.VMEM) for r in results])
    return ig, gw.T, uw.T, dw


def solution(mesh):
    placed = (
        P("tok", "inp"),
        P("inp", ("out", "tok")),
        P("inp", ("out", "tok")),
        P("tok", "inp"),
        P("inp", ("out", "tok")),
        P("inp", ("out", "tok")),
        P(("out", "tok"), "inp"),
    )
    return jax.shard_map(
        local,
        mesh=mesh,
        in_specs=placed,
        out_specs=(
            P(("out", "tok"), "inp"),
            P("inp", ("out", "tok")),
            P("inp", ("out", "tok")),
            P(("out", "tok"), "inp"),
        ),
        check_vma=False,
    )
```
